128 devices in a mesh: lon: 16 (over x, z_lo, core), lat: 8 (over z_hi, y).
Axes of the slice: x: 4, y: 4, z: 4 (z_hi: 2, z_lo: 2; z = z_hi * 2 + z_lo), core: 2. Of those that a mesh axis runs over, the one named last changes fastest.
Arguments:
- background: float32 [5, 32, 256, 2048], P(None, None, 'lat', 'lon'), may hold values from -6 to 6
- velocity: float32 [2, 32, 256, 2048], P(None, None, 'lat', 'lon'), may hold values from -0.22 to 0.22
- diffusivity: float32 [5], replicated, may hold values from 0.02 to 0.12
- obs_value: float32 [131072], P(('lon', 'lat')), may hold values from -6 to 6
- obs_weight: float32 [131072], P(('lon', 'lat')), may hold values from 0.25 to 4
- obs_owner: int32 [131072, 1], P(('lon', 'lat')), may hold values from 0 to 127; in each aligned block of 1024 rows (0 to 1023, 1024 to 2047, ...) at most 16 rows name the same one
- obs_counts: int32 [128, 8], P(('lon', 'lat')), may hold values from 1 to 128, 768 in all within a row
- obs_cell: int32 [131072], P(('lon', 'lat')), may hold values from 0 to 655359
Outputs:
- forecast: float32 [5, 32, 256, 2048], P(None, None, 'lat', 'lon')
- adjoint_state: float32 [5, 32, 256, 2048], P(None, None, 'lat', 'lon')
- departures: float32 [131072], P(('lon', 'lat'))
The draws below stay inside these ranges and needn't reach their ends.
Inputs may be any that keep to these rules, and one draw needn't show every extreme that they name: `obs_owner`: among the rows of one device, padding rows included, no slab is named more than 16 times, a bound that some block reaches. `obs_counts`: each device's 8 counts sum to 768; one of them is 128. `obs_cell`: index into the owner's slab, flattened over field, level, row and longitude.
All inputs are finite; a program needn't handle non-finite values.
Results may differ from the reference program's by a relative error of at most 0.00012.
Values sent between devices are 32-bit elements; how exact they have to be, the bound alone decides.
No kernel may reach another device: no remote copies, remote signals or barrier semaphores. Data moves between devices by JAX's collectives and lax.ppermute only.
A program may use at most 128 MiB of HBM per device.

```python
import math
import jax
import jax.numpy as jnp
import numpy as np

F = 5
K = 32
CL = 32
CW = 128
NBLK = 8
BLOCK_ROWS = 128
STEPS = 2
NLAT = 256
NLON = 2048
ROWS_DEV = 1024
OBS = 131072
CAP = 16
CELLS = 655360
N_LAT = 8
DEVICES = 128


def place_ends(values, rng, smallest, largest):
    shape = values.shape
    spot = [jax.random.randint(jax.random.fold_in(rng, axis), (), 0, shape[axis]) for axis in range(len(shape))]
    values = values.at[tuple(spot)].set(smallest)
    longest = shape.index(max(shape))
    spot[longest] = (spot[longest] + 1) % shape[longest]
    return values.at[tuple(spot)].set(largest)


def levels(rng, extent, split, low, high):
    def one(axis_at, parts):
        draws = jax.random.uniform(jax.random.fold_in(jax.random.fold_in(rng, 6), axis_at), (parts,), jnp.float32, low / len(split), high / len(split))
        return jnp.repeat(jnp.exp(draws), extent[axis_at] // parts).reshape((-1,) + (1,) * (len(extent) - axis_at - 1))

    factor_of = one(*split[0])
    for cut in split[1:]:
        factor_of = factor_of * one(*cut)
    return factor_of


def length_profile(number_of, total, bound, slope):
    portions = [(1 << 20) // math.isqrt(grade ** slope) + 1 for grade in range(2, number_of + 1)]
    spare, given = total - bound - (number_of - 1), [1] * (number_of - 1)
    while spare > 0:
        free = [i for i in range(number_of - 1) if given[i] < bound]
        mass, budget = sum([portions[i] for i in free]), spare
        for i in free:
            extra = min(bound - given[i], max(1, budget * portions[i] // mass), spare)
            given[i] = given[i] + extra
            spare = spare - extra
    return np.array([bound] + given)


def ragged(own_key, count, total, reach, slope):
    if count == 2:
        one = jax.random.randint(own_key, (), max(1, total - reach), min(reach, total - 1) + 1)
        return jnp.stack([one, total - one])
    tallies = jnp.asarray(length_profile(count, total, reach, slope), jnp.int32)
    twos = (count - 1) // 2
    source_of, taker = tallies[1:1 + 2 * twos:2], tallies[2:2 + 2 * twos:2]
    margin = jnp.minimum(source_of - 1, reach - taker)
    moved = jax.random.randint(jax.random.fold_in(own_key, 1), (twos,), 0, 1 << 20) % (margin + 1)
    tallies = tallies.at[1:1 + 2 * twos:2].set(source_of - moved).at[2:2 + 2 * twos:2].set(taker + moved)
    return tallies[jax.random.permutation(jax.random.fold_in(own_key, 2), count)]


def deal_out(stream_key, own, number, rows, amount, top, reach, skew):
    sequence = jax.random.permutation(stream_key, amount)
    packed, ordinary = portions_of(amount, rows * top, reach, skew, True), portions_of(amount, rows * top, reach, skew, False)
    places = jnp.arange(amount)

    def named(tallies, offset_by):
        used = int((tallies > 0).sum())
        fixed = max(1, used // 4)
        passed = fixed + (places - fixed + offset_by * (used - fixed)) % max(1, amount - fixed)
        return jnp.zeros((amount,), jnp.int32).at[sequence[jnp.where(places < fixed, places, passed)]].set(jnp.asarray(tallies, jnp.int32))

    tallies = jnp.where(number % 4 == 0, named(packed, number // 4), named(ordinary, number - number // 4 - 1))
    mixed = jax.random.permutation(jax.random.fold_in(own, 3), amount)
    donor, taker = mixed[0:amount // 2 * 2:2], mixed[1:amount // 2 * 2:2]
    room = jnp.minimum(tallies[donor] - 1, reach - tallies[taker]) // 2
    room = jnp.where((donor == sequence[0]) | (taker == sequence[0]) | (tallies[taker] == 0), 0, jnp.maximum(room, 0))
    passed = jax.random.randint(jax.random.fold_in(own, 4), (amount // 2,), 0, 1 << 20) % (room + 1)
    tallies = tallies.at[donor].add(-passed).at[taker].add(passed)
    items = jnp.searchsorted(jnp.cumsum(tallies), jnp.arange(rows * top), side="right").astype(jnp.int32)
    grid = items.reshape(top, rows).T
    grid = grid[jax.random.permutation(jax.random.fold_in(own, 1), rows)]
    offset_by = jax.random.randint(jax.random.fold_in(own, 2), (rows, 1), 0, top)
    return jnp.take_along_axis(grid, (jnp.arange(top)[None, :] + offset_by) % top, axis=1)


def portions_of(count, total, reach, slope, full):
    weights = [(1 << 20) // math.isqrt(rank ** slope) + 1 for rank in range(1, count + 1)]
    largest = reach if full else min(reach, max(-(-total // count), total * weights[0] // sum(weights)))
    least = 1 if total - largest >= count - 1 else 0
    given, spare = [largest] + [least] * (count - 1), total - largest - least * (count - 1)
    while spare > 0:
        candidates = [i for i in range(1, count) if given[i] < largest] or [i for i in range(1, count) if given[i] < reach]
        pool, remaining = sum([weights[i] for i in candidates]), spare
        for i in candidates:
            more = min(reach - given[i], max(1, remaining * weights[i] // pool), spare)
            given[i] = given[i] + more
            spare = spare - more
    return np.array(given)


def noise(rng, extent, scale, bound, split=(), kind=jnp.bfloat16):
    drawn = jax.random.normal(rng, extent, jnp.float32) * scale
    if len(split) > 0:
        drawn = levels(rng, extent, split, -0.22, 0.18) * drawn
    return jnp.clip(drawn, min=-bound, max=bound).astype(kind)


def setup_inputs(seed: int = 0) -> dict:
    seeds = jax.random.split(jax.random.key(seed), 9)
    background = noise(seeds[0], (F, K, NLAT, NLON), 1.0, 6.0, ((2, 8), (3, 16)), jnp.float32)
    velocity = jnp.clip(jax.random.uniform(seeds[1], (2, K, NLAT, NLON), jnp.float32, -0.22, 0.22) * levels(seeds[1], (2, K, NLAT, NLON), ((2, 8), (3, 16)), -0.4, 0.0), -0.22, 0.22)
    diffusivity = jnp.clip(jnp.exp(jax.random.uniform(seeds[2], (F,), jnp.float32, math.log(0.02), math.log(0.12))), 0.02, 0.12)
    obs_value = noise(seeds[3], (OBS,), 1.0, 6.0, ((0, 128),), jnp.float32)
    obs_weight = jnp.clip(jnp.exp(math.log(4.0) - 2.7725887 * jax.random.uniform(seeds[4], (OBS,), jnp.float32) ** levels(seeds[4], (OBS,), ((0, 128),), -0.2, 0.2)), 0.25, 4.0)
    obs_owner_keys = jax.random.split(jax.random.fold_in(seeds[5], 1), OBS // ROWS_DEV)
    obs_owner_turns = jax.random.permutation(jax.random.fold_in(seeds[5], 3), OBS // ROWS_DEV)
    obs_owner = jax.vmap(lambda own, number: deal_out(jax.random.fold_in(seeds[5], 2), own, number, ROWS_DEV, DEVICES, 1, CAP, 2))(obs_owner_keys, obs_owner_turns).reshape((OBS, 1))
    obs_counts = jax.vmap(lambda own: ragged(own, NBLK, 96 * NBLK, BLOCK_ROWS, 1))(jax.random.split(seeds[6], DEVICES)).reshape((DEVICES, NBLK)).astype(jnp.int32)
    obs_cell = place_ends(jax.random.randint(seeds[7], (OBS,), 0, CELLS), jax.random.fold_in(seeds[7], 1), 0, CELLS - 1).astype(jnp.int32)
    return {"background": background, "velocity": velocity, "diffusivity": diffusivity, "obs_value": obs_value, "obs_weight": obs_weight, "obs_owner": obs_owner, "obs_counts": obs_counts, "obs_cell": obs_cell}


FLIP_SIGNS = (1.0, 1.0, -1.0, -1.0, 1.0)


def neighbours(field, flip):
    from_east = jnp.roll(field, -1, axis=-1)
    from_west = jnp.roll(field, 1, axis=-1)
    from_south = jnp.concatenate([jnp.zeros_like(field[..., :1, :]), field[..., :-1, :]], axis=-2)
    from_north = jnp.concatenate([field[..., 1:, :], flip * field[..., -1:, ::-1]], axis=-2)
    return from_west, from_east, from_south, from_north


def reference(background, velocity, diffusivity, obs_value, obs_weight, obs_owner, obs_counts, obs_cell):
    flip = jnp.array(FLIP_SIGNS, dtype=jnp.float32)[:, None, None, None]
    eastward = velocity[0]
    northward = velocity[1]
    diffuse = diffusivity[:, None, None, None]
    centre = 1.0 - 4.0 * diffuse - jnp.abs(eastward) - jnp.abs(northward)

    def forward_step(field):
        from_west, from_east, from_south, from_north = neighbours(field, flip)
        return (centre * field + (diffuse - jnp.minimum(eastward, 0.0)) * from_east
                + (diffuse + jnp.maximum(eastward, 0.0)) * from_west
                + (diffuse - jnp.minimum(northward, 0.0)) * from_north
                + (diffuse + jnp.maximum(northward, 0.0)) * from_south)

    east_at_west, east_at_east, _, _ = neighbours(eastward, 1.0)
    _, _, north_at_south, north_at_north = neighbours(northward, 1.0)
    upper = jnp.concatenate([jnp.maximum(north_at_north[:, :-1, :], 0.0),
                             -jnp.minimum(north_at_north[:, -1:, :], 0.0)], axis=1)

    def adjoint_step(adjoint):
        from_west, from_east, from_south, from_north = neighbours(adjoint, flip)
        return (centre * adjoint + (diffuse - jnp.minimum(east_at_west, 0.0)) * from_west
                + (diffuse + jnp.maximum(east_at_east, 0.0)) * from_east
                + (diffuse - jnp.minimum(north_at_south, 0.0)) * from_south
                + (diffuse + upper) * from_north)

    states = [background]
    for step in range(STEPS):
        states.append(forward_step(states[-1]))

    all_rows = obs_value.shape[0]
    row_index = jnp.arange(all_rows, dtype=jnp.int32)
    device_of = row_index // ROWS_DEV
    local_row = row_index % ROWS_DEV
    block_index = local_row // BLOCK_ROWS
    position = local_row % BLOCK_ROWS
    is_live = position < obs_counts[device_of, block_index]
    obs_time = block_index % (STEPS + 1)
    owner_id = obs_owner[:, 0]
    field_of = obs_cell // (K * CL * CW)
    level_of = (obs_cell // (CL * CW)) % K
    row_of = (obs_cell // CW) % CL
    column_of = obs_cell % CW
    global_row = (owner_id % N_LAT) * CL + row_of
    global_column = (owner_id // N_LAT) * CW + column_of
    flat_index = ((field_of * K + level_of) * NLAT + global_row) * NLON + global_column
    flat_index = flat_index.astype(jnp.int32)
    modelled = jnp.zeros(obs_value.shape, dtype=jnp.float32)
    for step in range(STEPS + 1):
        modelled = jnp.where(obs_time == step, states[step].reshape(-1)[flat_index], modelled)
    weight = jnp.where(is_live, obs_weight, 0.0)
    departure = weight * (obs_value - modelled)
    total_cells = background.size

    def forcing(step):
        spread = jax.ops.segment_sum(jnp.where(obs_time == step, departure, 0.0), flat_index,
                                     num_segments=total_cells)
        return spread.reshape(background.shape)

    adjoint = forcing(STEPS)
    for step in range(STEPS - 1, -1, -1):
        adjoint = adjoint_step(adjoint) + forcing(step)
    return states[-1], adjoint, departure
```

```python
import jax
import jax.numpy as jnp
from jax import lax
from jax.experimental import pallas as pl
from jax.experimental.pallas import tpu as pltpu
from jax.sharding import PartitionSpec as P


STEPS = 2
F = 5
K = 32
CL = 32
CW = 128
PLANES = F * K
ALL = PLANES + 2 * K
EXT = 40
ROWS = PLANES * CL
NBLK = 8
NDEV = 128
CAP = 16
MIB = 1 << 20
f32 = jnp.float32
i32 = jnp.int32
HIGHEST = lax.Precision.HIGHEST


def iota(shape, dim):
    return lax.broadcasted_iota(i32, shape, dim)


def call(body, outs, ins, name, scratch=(), vmem=48, flops=10**6, nbytes=10**6):
    return pl.pallas_call(
        body,
        out_shape=[jax.ShapeDtypeStruct(shape, dtype) for shape, dtype in outs],
        in_specs=[pl.BlockSpec(memory_space=space) for space, _ in ins],
        out_specs=[pl.BlockSpec(memory_space=pltpu.VMEM)] * len(outs),
        scratch_shapes=list(scratch),
        compiler_params=pltpu.CompilerParams(vmem_limit_bytes=vmem * MIB),
        cost_estimate=pl.CostEstimate(flops=flops, bytes_accessed=nbytes, transcendentals=0),
        name=name,
    )(*[x for _, x in ins])


V = pltpu.VMEM
S = pltpu.SMEM


def reverse_lanes(x):
    return jnp.take_along_axis(x, 127 - iota(x.shape, 1), axis=1)


def fold_sign(planes):
    kind = iota((planes, CW), 0) // K
    return jnp.where((kind == 2) | (kind == 3) | (kind >= F), -1.0, 1.0).astype(f32)


def rows_kernel(meta, x, vel, pay1, pay2):
    odd = meta[0] == 1
    for d in range(2):
        for ref, count, base in ((x, PLANES, 0), (vel, 2 * K, PLANES)):
            low = ref[pl.ds(d, count, stride=CL), :]
            high = ref[pl.ds(CL - 1 - d, count, stride=CL), :]
            pay1[d, base : base + count, :] = jnp.where(odd, low, high)
            pay2[d, base : base + count, :] = jnp.where(odd, high, low)

    @pl.when(meta[1] == 1)
    def _():
        sign = fold_sign(ALL)
        for d in range(2):
            pay2[d] = sign * reverse_lanes(pay2[d])


def fill_edge(edge, got1, got2, odd, planes, base=0):
    for d in range(2):
        one = got1[d, base : base + planes, :]
        two = got2[d, base : base + planes, :]
        edge[pl.ds(d, planes, stride=8), :] = jnp.where(odd, two, one)
        edge[pl.ds(7 - d, planes, stride=8), :] = jnp.where(odd, one, two)


def clear(ref, step=256):
    rows = ref.shape[0]

    @pl.loop(0, rows // step)
    def _(i):
        ref[pl.ds(i * step, step), :] = jnp.zeros((step, CW), f32)


def tile(ref, plane, height, base=0):
    return ref[pl.ds(pl.multiple_of(base + plane * height, 8), height), :]


def columns_kernel(meta, x, vel, got1, got2, own, edge):
    clear(edge)
    fill_edge(edge, got1, got2, meta[0] == 1, ALL)
    own[...] = jnp.zeros(own.shape, f32)
    group = iota((EXT, CW), 1) >> 2

    @pl.loop(0, K)
    def _(level):
        here = group == level
        for kind in range(F + 2):
            ref, plane = (x, kind * K) if kind < F else (vel, (kind - F) * K)
            full = jnp.concatenate(
                [tile(ref, plane + level, CL), tile(edge, kind * K + level, 8)], axis=0
            )
            moved = pltpu.roll(full, 4 * level + 2, axis=1)
            own[kind] = jnp.where(here, moved, own[kind])


def north(x):
    return pltpu.roll(x, EXT - 1, axis=0)


def south(x):
    return pltpu.roll(x, 1, axis=0)


def east(x):
    return pltpu.roll(x, CW - 1, axis=1)


def west(x):
    return pltpu.roll(x, 1, axis=1)


def parts(u, v):
    return (
        1.0 - jnp.abs(u) - jnp.abs(v),
        -jnp.minimum(u, 0.0),
        jnp.maximum(u, 0.0),
        -jnp.minimum(v, 0.0),
        jnp.maximum(v, 0.0),
    )


def forward_kernel(meta, kap, x, vel, got1, got2, own, from_west, from_east, states, forecast,
                   edge, side, side1):
    bottom = meta[2] == 1
    clear(edge)
    fill_edge(edge, got1, got2, meta[0] == 1, ALL)
    lane = iota((EXT, CW), 1)
    row = iota((EXT, CW), 0)
    slot = lane & 3
    for kind in range(F + 2):
        side[kind] = jnp.where(slot < 2, from_west[kind], from_east[kind])
    base, um, up, vm, vp = parts(side[F], side[F + 1])
    for f in range(F):
        k = kap[f]
        mine = own[f]
        near = side[f]
        e = jnp.where(slot == 1, east(mine), east(near))
        w = jnp.where(slot == 1, west(near), west(mine))
        side1[f] = (
            (base - 4.0 * k) * near
            + (k + um) * e
            + (k + up) * w
            + (k + vm) * north(near)
            + (k + vp) * south(near)
        )
    first = lane == 0
    last = lane == CW - 1
    gone = bottom & (row >= CL + 2)

    @pl.loop(0, K)
    def _(level):
        def whole(ref, kind, offset):
            return jnp.concatenate(
                [tile(ref, (kind - offset) * K + level, CL), tile(edge, kind * K + level, 8)], axis=0
            )

        u = whole(vel, F, F)
        v = whole(vel, F + 1, F)
        base, um, up, vm, vp = parts(u, v)
        for f in range(F):
            k = kap[f]
            ce = base - 4.0 * k
            cu, cw, cn, cs = k + um, k + up, k + vm, k + vp
            a = whole(x, f, 0)
            h = pltpu.roll(side[f], 126 - 4 * level, axis=1)
            b = (
                ce * a
                + cu * east(jnp.where(first, h, a))
                + cw * west(jnp.where(last, h, a))
                + cn * north(a)
                + cs * south(a)
            )
            b = jnp.where(gone, 0.0, b)
            h = pltpu.roll(side1[f][:CL], 126 - 4 * level, axis=1)
            main = b[:CL]
            c = (
                ce[:CL] * main
                + cu[:CL] * east(jnp.where(first[:CL], h, main))
                + cw[:CL] * west(jnp.where(last[:CL], h, main))
                + cn[:CL] * north(b)[:CL]
                + cs[:CL] * south(b)[:CL]
            )
            at = pl.multiple_of((f * K + level) * CL, CL)
            states[pl.ds(at, CL), :] = a[:CL]
            states[pl.ds(ROWS + at, CL), :] = main
            states[pl.ds(2 * ROWS + at, CL), :] = c
            forecast[pl.ds(at, CL), :] = c


def pack_kernel(counts, value, weight, owner, cell, pay, slots):
    dest = iota((NDEV, 128), 0)
    lane = iota((1, 128), 1)
    before = (iota((128, 128), 0) < iota((128, 128), 1)).astype(f32).astype(jnp.bfloat16)
    ones = jnp.ones((128, 128), jnp.bfloat16)
    carry = jnp.zeros((NDEV, 128), f32)
    total = jnp.zeros((NDEV, 128), f32)
    place = iota((CAP, 128), 0).astype(f32)
    for b in range(NBLK):
        live = lane < counts[0, b]
        who = jnp.where(live, owner[b : b + 1, :], -1)
        hot = (dest == who).astype(f32)
        hot16 = hot.astype(jnp.bfloat16)
        earlier = carry + jnp.dot(hot16, before, preferred_element_type=f32)
        carry = carry + jnp.dot(hot16, ones, preferred_element_type=f32)
        slot = jnp.sum(hot * earlier, axis=0, keepdims=True)
        slot = jnp.where(live, slot, -1.0)
        slots[b : b + 1, :] = slot
        c = cell[b : b + 1, :]
        line = ((c >> 7) + (b % (STEPS + 1)) * ROWS).astype(f32)
        column = (c & 127).astype(f32)
        here = place == slot
        fields = [
            jnp.where(here, data, 0.0)
            for data in (value[b : b + 1, :], weight[b : b + 1, :], line, column)
        ]
        fields.append(jnp.zeros((128 - 4 * CAP, 128), f32))
        total = total + lax.dot_general(
            hot,
            jnp.concatenate(fields, axis=0),
            (((1,), (1,)), ((), ())),
            precision=HIGHEST,
            preferred_element_type=f32,
        )
    pay[...] = total


GROUP = 8


def adjoint_kernel(meta, kap, arrived, states, vel, got1, got2, own_v, from_west, from_east,
                   departures, out, out_edge, spill,
                   forcing, rows_of, adds, index_v, index_s, edge, first_adj, own_f, own_a, zside):
    bottom = meta[2] == 1
    box = arrived[...]
    flat = jnp.transpose(box)
    index_v[...] = flat[2 * CAP : 3 * CAP].astype(i32)
    pltpu.sync_copy(index_v, index_s)
    clear(forcing)
    clear(edge)
    fill_edge(edge, got1, got2, meta[0] == 1, 2 * K, PLANES)

    @pl.loop(0, NDEV)
    def _(s):
        for q in range(CAP):
            at = index_s[q, s]
            rows_of[pl.ds(q * NDEV + s, 1), :] = states[pl.ds(at, 1), :]

    lane_s = iota((NDEV, CW), 1)
    lane_f = lane_s.astype(f32)
    result = jnp.zeros((NDEV, CW), f32)
    for start in range(0, CAP, GROUP):
        for q in range(start, start + GROUP):
            spot = lane_f == box[:, 3 * CAP + q : 3 * CAP + q + 1]
            seen = rows_of[q * NDEV : (q + 1) * NDEV, :]
            modelled = jnp.sum(jnp.where(spot, seen, 0.0), axis=1, keepdims=True)
            dep = box[:, CAP + q : CAP + q + 1] * (box[:, q : q + 1] - modelled)
            result = jnp.where(lane_s == q, dep, result)
            adds[q * NDEV : (q + 1) * NDEV, :] = jnp.where(spot, dep, 0.0)
        for q in range(start + GROUP - 1, start, -1):
            mine = box[:, 2 * CAP + q : 2 * CAP + q + 1]
            acc = adds[q * NDEV : (q + 1) * NDEV, :]
            for p in range(start, q):
                same = jnp.broadcast_to(mine == box[:, 2 * CAP + p : 2 * CAP + p + 1], (NDEV, CW))
                acc = acc + jnp.where(same, adds[p * NDEV : (p + 1) * NDEV, :], 0.0)
            adds[q * NDEV : (q + 1) * NDEV, :] = acc
    departures[...] = result

    @pl.loop(0, NDEV)
    def _(s):
        for start in range(0, CAP, GROUP):
            ats = [index_s[q, s] for q in range(start, start + GROUP)]
            olds = [forcing[pl.ds(at, 1), :] for at in ats]
            for n in range(GROUP):
                forcing[pl.ds(ats[n], 1), :] = (
                    olds[n] + adds[pl.ds((start + n) * NDEV + s, 1), :]
                )

    lane = iota((EXT, CW), 1)
    row = iota((EXT, CW), 0)
    first = lane == 0
    last = lane == CW - 1
    gone = bottom & (row >= CL + 2)
    group = lane >> 2
    slot = lane & 3
    nothing = jnp.zeros((8, CW), f32)
    own_f[...] = jnp.zeros(own_f.shape, f32)
    own_a[...] = jnp.zeros(own_a.shape, f32)

    def velocity_of(level):
        return [
            jnp.concatenate([tile(vel, n * K + level, CL), tile(edge, n * K + level, 8)], axis=0)
            for n in range(2)
        ]

    @pl.loop(0, K)
    def _(level):
        base, um, up, vm, vp = parts(*velocity_of(level))
        here = group == level
        for f in range(F):
            k = kap[f]
            at = f * K + level
            a = jnp.concatenate([tile(forcing, at, CL, 2 * ROWS), nothing], axis=0)
            own_f[f] = jnp.where(here, pltpu.roll(a, 4 * level + 2, axis=1), own_f[f])
            b = (
                (base - 4.0 * k) * a
                + jnp.where(first, 0.0, west((k + um) * a))
                + jnp.where(last, 0.0, east((k + up) * a))
                + south((k + vm) * a)
                + north((k + vp) * a)
            )
            b = jnp.where(gone, 0.0, b)
            b = b + jnp.concatenate([tile(forcing, at, CL, ROWS), nothing], axis=0)
            own_a[f] = jnp.where(here, pltpu.roll(b, 4 * level + 2, axis=1), own_a[f])
            first_adj[pl.ds(pl.multiple_of(at * EXT, 8), EXT), :] = b

    su, sv = [jnp.where(slot < 2, from_west[n], from_east[n]) for n in range(2)]
    base, um, up, vm, vp = parts(su, sv)
    _, oum, oup, _, _ = parts(own_v[0], own_v[1])
    for f in range(F):
        k = kap[f]
        b = jnp.where(
            slot == 1,
            east((k + oup) * own_f[f]),
            jnp.where(slot == 2, west((k + oum) * own_f[f]), 0.0),
        )
        pa = (k + um) * b
        pb = (k + up) * b
        zside[f] = jnp.where(slot == 1, pa, pb)
        inner = (
            (base - 4.0 * k) * b
            + south((k + vm) * b)
            + north((k + vp) * b)
            + jnp.where(slot == 1, east((k + oup) * own_a[f]), west((k + oum) * own_a[f]))
        )
        outer = jnp.where(slot == 0, east(pb), west(pa))
        spill[f] = jnp.where((slot == 1) | (slot == 2), inner, outer)

    @pl.loop(0, K)
    def _(level):
        base, um, up, vm, vp = parts(*velocity_of(level))
        for f in range(F):
            k = kap[f]
            at = f * K + level
            a = tile(first_adj, at, EXT)
            h = pltpu.roll(zside[f], 126 - 4 * level, axis=1)
            b = (
                (base - 4.0 * k) * a
                + west(jnp.where(last, h, (k + um) * a))
                + east(jnp.where(first, h, (k + up) * a))
                + south((k + vm) * a)
                + north((k + vp) * a)
            )
            out[pl.ds(pl.multiple_of(at * CL, CL), CL), :] = b[:CL] + tile(forcing, at, CL)
            out_edge[pl.ds(pl.multiple_of(at * 8, 8), 8), :] = b[CL:]


def edge_kernel(meta, out_edge, from_west, from_east, pay1, pay2, edge):
    odd = meta[0] == 1
    lane = iota((8, CW), 1)
    slot = lane & 3
    close = (lane < 2) | (lane >= CW - 2)
    merged = [
        jnp.where(slot < 2, from_east[f, CL:EXT, :], from_west[f, CL:EXT, :]) for f in range(F)
    ]

    @pl.loop(0, K)
    def _(level):
        for f in range(F):
            more = pltpu.roll(merged[f], 126 - 4 * level, axis=1)
            at = pl.multiple_of((f * K + level) * 8, 8)
            edge[pl.ds(at, 8), :] = out_edge[pl.ds(at, 8), :] + jnp.where(close, more, 0.0)

    for d in range(2):
        up = edge[pl.ds(d, PLANES, stride=8), :]
        down = edge[pl.ds(7 - d, PLANES, stride=8), :]
        pay1[d] = jnp.where(odd, down, up)
        pay2[d] = jnp.where(odd, up, down)

    @pl.when(meta[1] == 1)
    def _():
        sign = fold_sign(PLANES)
        for d in range(2):
            pay2[d] = sign * reverse_lanes(pay2[d])


def finish_kernel(meta, part, from_west, from_east, got1, got2, returned, owner, slots,
                  adjoint, departures):
    odd = meta[0] == 1
    lane = iota((CL, CW), 1)
    slot = lane & 3
    close = (lane < 2) | (lane >= CW - 2)
    merged = [jnp.where(slot < 2, from_east[f, :CL, :], from_west[f, :CL, :]) for f in range(F)]

    @pl.loop(0, K)
    def _(level):
        for f in range(F):
            more = pltpu.roll(merged[f], 126 - 4 * level, axis=1)
            at = pl.multiple_of((f * K + level) * CL, CL)
            adjoint[pl.ds(at, CL), :] = part[pl.ds(at, CL), :] + jnp.where(close, more, 0.0)

    for d in range(2):
        up = pl.ds(CL - 1 - d, PLANES, stride=CL)
        adjoint[up, :] = adjoint[up, :] + jnp.where(odd, got2[d], got1[d])
        down = pl.ds(d, PLANES, stride=CL)
        adjoint[down, :] = adjoint[down, :] + jnp.where(odd, got1[d], got2[d])

    flat = jnp.transpose(returned[...])[:CAP]
    dest = iota((NDEV, 128), 0)
    place = iota((CAP, 128), 0).astype(f32)
    for b in range(NBLK):
        hot = (dest == owner[b : b + 1, :]).astype(f32)
        found = jnp.dot(flat, hot, precision=HIGHEST, preferred_element_type=f32)
        departures[b : b + 1, :] = jnp.sum(
            jnp.where(place == slots[b : b + 1, :], found, 0.0), axis=0, keepdims=True
        )


def all_to_all(x):
    x = x.reshape(NDEV, 1, 128)
    x = lax.all_to_all(x, ("lon", "lat"), split_axis=0, concat_axis=0, tiled=True)
    return x.reshape(NDEV, 128)


def shards(
    background, velocity, diffusivity, obs_value, obs_weight, obs_owner, obs_counts, obs_cell
):
    nlon = lax.axis_size("lon")
    nlat = lax.axis_size("lat")
    both = ("lon", "lat")
    at = lax.axis_index("lat")
    meta = jnp.stack([at & 1, (at == nlat - 1).astype(i32), (at == 0).astype(i32)])

    def number(i, j):
        return i * nlat + j

    pairs1 = [(number(i, j), number(i, j ^ 1)) for i in range(nlon) for j in range(nlat)]
    pairs2 = []
    for i in range(nlon):
        for j in range(1, nlat - 1):
            pairs2.append((number(i, j), number(i, j + 1 if j & 1 else j - 1)))
        pairs2.append((number(i, nlat - 1), number(nlon - 1 - i, nlat - 1)))
    eastward = [(i, (i + 1) % nlon) for i in range(nlon)]
    westward = [((i + 1) % nlon, i) for i in range(nlon)]

    def around(x):
        return lax.ppermute(x, "lon", eastward), lax.ppermute(x, "lon", westward)

    x = background.reshape(ROWS, CW)
    vel = velocity.reshape(2 * K * CL, CW)
    pay1, pay2 = call(
        rows_kernel,
        [((2, ALL, CW), f32)] * 2,
        [(S, meta), (V, x), (V, vel)],
        "rows",
    )
    got1 = lax.ppermute(pay1, both, pairs1)
    got2 = lax.ppermute(pay2, both, pairs2)

    owner = obs_owner.reshape(NBLK, 128)
    packed, slots = call(
        pack_kernel,
        [((NDEV, 128), f32), ((NBLK, 128), f32)],
        [
            (S, obs_counts),
            (V, obs_value.reshape(NBLK, 128)),
            (V, obs_weight.reshape(NBLK, 128)),
            (V, owner),
            (V, obs_cell.reshape(NBLK, 128)),
        ],
        "pack",
    )
    (own,) = call(
        columns_kernel,
        [((F + 2, EXT, CW), f32)],
        [(S, meta), (V, x), (V, vel), (V, got1), (V, got2)],
        "columns",
        scratch=[V((ALL * 8, CW), f32)],
    )
    from_west, from_east = around(own)
    arrived = all_to_all(packed)
    states, forecast = call(
        forward_kernel,
        [((3 * ROWS, CW), f32), ((ROWS, CW), f32)],
        [
            (S, meta),
            (S, diffusivity),
            (V, x),
            (V, vel),
            (V, got1),
            (V, got2),
            (V, own),
            (V, from_west),
            (V, from_east),
        ],
        "forward",
        scratch=[
            V((ALL * 8, CW), f32),
            V((F + 2, EXT, CW), f32),
            V((F, EXT, CW), f32),
        ],
    )
    departures, part, part_edge, spill = call(
        adjoint_kernel,
        [
            ((NDEV, 128), f32),
            ((ROWS, CW), f32),
            ((PLANES * 8, CW), f32),
            ((F, EXT, CW), f32),
        ],
        [
            (S, meta),
            (S, diffusivity),
            (V, arrived),
            (V, states),
            (V, vel),
            (V, got1),
            (V, got2),
            (V, own[F:]),
            (V, from_west[F:]),
            (V, from_east[F:]),
        ],
        "adjoint",
        scratch=[
            V((3 * ROWS, CW), f32),
            V((CAP * NDEV, CW), f32),
            V((CAP * NDEV, CW), f32),
            V((CAP, 128), i32),
            S((CAP, 128), i32),
            V((2 * K * 8, CW), f32),
            V((PLANES * EXT, CW), f32),
            V((F, EXT, CW), f32),
            V((F, EXT, CW), f32),
            V((F, EXT, CW), f32),
        ],
    )
    spill_west, spill_east = around(spill)
    returned = all_to_all(departures)
    pay1, pay2 = call(
        edge_kernel,
        [((2, PLANES, CW), f32)] * 2,
        [(S, meta), (V, part_edge), (V, spill_west), (V, spill_east)],
        "edge",
        scratch=[V((PLANES * 8, CW), f32)],
    )
    back1 = lax.ppermute(pay1, both, pairs1)
    back2 = lax.ppermute(pay2, both, pairs2)
    adjoint, found = call(
        finish_kernel,
        [((ROWS, CW), f32), ((NBLK, 128), f32)],
        [
            (S, meta),
            (V, part),
            (V, spill_west),
            (V, spill_east),
            (V, back1),
            (V, back2),
            (V, returned),
            (V, owner),
            (V, slots),
        ],
        "finish",
    )
    shape = (F, K, CL, CW)
    return forecast.reshape(shape), adjoint.reshape(shape), found.reshape(-1)


def solution(mesh):
    in_specs = (
        P(None, None, "lat", "lon"),
        P(None, None, "lat", "lon"),
        P(),
        P(("lon", "lat")),
        P(("lon", "lat")),
        P(("lon", "lat"), None),
        P(("lon", "lat"), None),
        P(("lon", "lat")),
    )
    out_specs = (P(None, None, "lat", "lon"), P(None, None, "lat", "lon"), P(("lon", "lat")))
    return jax.shard_map(shards, mesh=mesh, in_specs=in_specs, out_specs=out_specs, check_vma=False)
```

```python
import jax
import jax.numpy as jnp
from jax import lax
from jax.experimental import pallas as pl
from jax.experimental.pallas import tpu as pltpu
from jax.sharding import PartitionSpec as P


STEPS = 2
F = 5
K = 32
CL = 32
CW = 128
PLANES = F * K
ALL = PLANES + 2 * K
EXT = 40
ROWS = PLANES * CL
NBLK = 8
NDEV = 128
CAP = 16
MIB = 1 << 20
f32 = jnp.float32
i32 = jnp.int32


V = pltpu.VMEM
S = pltpu.SMEM
H = pltpu.HBM


def iota(shape, dim):
    return lax.broadcasted_iota(i32, shape, dim)


def call(body, outs, ins, name, scratch=(), vmem=53, flops=10**6, nbytes=10**6):
    return pl.pallas_call(
        body,
        out_shape=[jax.ShapeDtypeStruct(shape, dtype) for shape, dtype, *_ in outs],
        in_specs=[pl.BlockSpec(memory_space=space) for space, _ in ins],
        out_specs=[pl.BlockSpec(memory_space=out[2] if len(out) > 2 else V) for out in outs],
        scratch_shapes=list(scratch),
        compiler_params=pltpu.CompilerParams(vmem_limit_bytes=vmem * MIB),
        cost_estimate=pl.CostEstimate(flops=flops, bytes_accessed=nbytes, transcendentals=0),
        name=name,
    )(*[x for _, x in ins])


def reverse_lanes(x):
    return jnp.take_along_axis(x, 127 - iota(x.shape, 1), axis=1)


def fold_sign(planes):
    kind = iota((planes, CW), 0) // K
    return jnp.where((kind == 2) | (kind == 3) | (kind >= F), -1.0, 1.0).astype(f32)


def where_am_i():
    at = lax.axis_index("lat")
    return at & 1 == 1, at == lax.axis_size("lat") - 1, at == 0


def partners():
    i, j = lax.axis_index("lon"), lax.axis_index("lat")
    n, m = lax.axis_size("lon"), lax.axis_size("lat")
    top = j == m - 1
    to_east, to_west = lax.rem(i + 1, n), lax.rem(i + n - 1, n)
    north_of, south_of = jnp.minimum(j + 1, m - 1), jnp.maximum(j - 1, 0)
    return (
        jnp.where(top, lax.rem(2 * n - 2 - i, n), to_east) * m + north_of,
        jnp.where(top, lax.rem(n - i, n), to_west) * m + north_of,
        to_east * m + south_of,
        to_west * m + south_of,
    )


def corner_rows(blocks, line, place):
    slot = iota((8, CW), 1) & 3
    rows = []
    for start in range(0, len(blocks), 4):
        row = jnp.zeros((8, CW), f32)
        for kind, block in enumerate(blocks[start : start + 4]):
            row = jnp.where(slot == kind, pltpu.roll(block, (kind - place) % CW, axis=1), row)
        rows.append(row[line : line + 1])
    return rows


def post_corners(pay, rows, bottom):
    for n, at in enumerate(partners()):
        for r in range(2):
            @pl.when(jnp.logical_not(bottom) if n >= 2 else at >= 0)
            def _(n=n, at=at, r=r):
                pay[pl.ds(MESSAGE * at + 1 + r, 1), :] = rows[n][r]


def corner_line(got, kind, first, second):
    slot = iota((8, CW), 1) & 3
    ats = partners()
    line = jnp.zeros((8, CW), f32)
    for place, n in ((1, first), (2, second)):
        row = got[pl.ds(MESSAGE * ats[n] + 1 + kind // 4, 1), :]
        moved = pltpu.roll(jnp.broadcast_to(row, (8, CW)), (place - kind % 4) % CW, axis=1)
        line = jnp.where(slot == place, moved, line)
    return line[:1]


NE, NW, SE, SW = range(4)
MESSAGE = 3
FLIPPED = (2, 3, 5, 6)


def thirds(x):
    pieces = []
    for _ in range(3):
        piece = x.astype(jnp.bfloat16)
        pieces.append(piece)
        x = x - piece.astype(f32)
    return pieces


def edges_kernel(x, vel, own, pay1, pay2, held, sems):
    odd, top, _ = where_am_i()
    copies = []
    for kind in range(F + 2):
        ref, plane = (x, kind * K) if kind < F else (vel, (kind - F) * K)
        copies.append(
            pltpu.make_async_copy(
                ref.at[pl.ds(plane * CL, K * CL)],
                held.at[pl.ds(kind * K * CL, K * CL)],
                sems.at[kind],
            )
        )
    for copy in copies:
        copy.start()
    group = iota((CL, CW), 1) >> 2
    for kind in range(F + 2):
        copies[kind].wait()
        for d in range(2 if kind < F else 1):
            low = held[pl.ds(kind * K * CL + d, K, stride=CL), :]
            high = held[pl.ds(kind * K * CL + CL - 1 - d, K, stride=CL), :]
            to = slice(d * ALL + kind * K, d * ALL + kind * K + K)
            pay1[to, :] = jnp.where(odd, low, high)
            pay2[to, :] = jnp.where(odd, high, low)

        def step(level, packed):
            rows = held[pl.ds(pl.multiple_of((kind * K + level) * CL, CL), CL), :]
            moved = pltpu.roll(rows, 4 * level + 2, axis=1)
            return jnp.where(group == level, moved, packed)

        own[kind] = lax.fori_loop(0, K, step, jnp.zeros((CL, CW), f32), unroll=True)

    @pl.when(top)
    def _():
        pay2[:ALL, :] = fold_sign(ALL) * reverse_lanes(pay2[:ALL, :])
        pay2[ALL:, :] = fold_sign(PLANES) * reverse_lanes(pay2[ALL:, :])


def halo_rows(got1, got2, odd):
    near, far = slice(0, ALL), slice(ALL, ALL + PLANES)
    norths = [jnp.where(odd, got2[cut, :], got1[cut, :]) for cut in (near, far)]
    souths = [jnp.where(odd, got1[cut, :], got2[cut, :]) for cut in (near, far)]
    return norths + souths


def spread(line):
    level, lane = iota((K, CW), 0), iota((K, CW), 1)
    return jnp.take_along_axis(
        jnp.broadcast_to(line, (K, CW)), (lane + 4 * level + 2) & (CW - 1), axis=1
    )


def gather_line(rows):
    level, lane = iota((K, CW), 0), iota((K, CW), 1)
    moved = jnp.take_along_axis(rows, (lane - 4 * level - 2) & (CW - 1), axis=1)
    return jnp.sum(jnp.where(lane >> 2 == level, moved, 0.0), axis=0, keepdims=True)


def north(x):
    return pltpu.roll(x, EXT - 1, axis=0)


def south(x):
    return pltpu.roll(x, 1, axis=0)


def east(x):
    return pltpu.roll(x, CW - 1, axis=1)


def west(x):
    return pltpu.roll(x, 1, axis=1)


def swapped(x, slot):
    return jnp.where(slot == 1, east(x), jnp.where(slot == 2, west(x), x))


def parts(u, v):
    return (
        1.0 - jnp.abs(u) - jnp.abs(v),
        -jnp.minimum(u, 0.0),
        jnp.maximum(u, 0.0),
        -jnp.minimum(v, 0.0),
        jnp.maximum(v, 0.0),
    )


def pack_kernel(counts, value, weight, owner, cell, own, pay, slots):
    dest = iota((NDEV, 128), 0)
    lane = iota((1, 128), 1)
    before = (iota((128, 128), 0) < iota((128, 128), 1)).astype(f32).astype(jnp.bfloat16)
    ones = jnp.ones((128, 128), jnp.bfloat16)
    carry = jnp.zeros((NDEV, 128), f32)
    total = jnp.zeros((NDEV, 128), f32)
    place = iota((CAP, 128), 0).astype(f32)
    for b in range(NBLK):
        live = lane < counts[0, b]
        who = jnp.where(live, owner[b : b + 1, :], -1)
        hot = (dest == who).astype(f32)
        hot16 = hot.astype(jnp.bfloat16)
        earlier = carry + jnp.dot(hot16, before, preferred_element_type=f32)
        carry = carry + jnp.dot(hot16, ones, preferred_element_type=f32)
        slot = jnp.sum(hot * earlier, axis=0, keepdims=True)
        slot = jnp.where(live, slot, -1.0)
        slots[b : b + 1, :] = slot
        code = (cell[b : b + 1, :] + (b % (STEPS + 1)) * (ROWS * CW)).astype(f32)
        here = place == slot
        fields = [
            jnp.where(here, data, 0.0) for data in (value[b : b + 1, :], weight[b : b + 1, :], code)
        ]
        fields.append(jnp.zeros((128 - 3 * CAP, 128), f32))
        total = total + lax.dot_general(
            jnp.concatenate([hot16] * 3, axis=1),
            jnp.concatenate(thirds(jnp.concatenate(fields, axis=0)), axis=1),
            (((1,), (1,)), ((), ())),
            preferred_element_type=f32,
        )
    pay[...] = jnp.zeros(pay.shape, f32)
    pay[pl.ds(0, NDEV, stride=MESSAGE), :] = total
    low = [own[kind, :8, :] for kind in range(F + 2)]
    high = [own[kind, CL - 8 :, :] for kind in range(F + 2)]
    _, _, bottom = where_am_i()
    post_corners(
        pay,
        [
            corner_rows(high, 7, 1),
            corner_rows(high, 7, 2),
            corner_rows(low, 0, 1),
            corner_rows(low, 0, 2),
        ],
        bottom,
    )


PAD = 8
GROUP = 8
UNROLL = 4
TILES = CL // 8


def core_kernel(kap, arrived, x, vel_in, got1, got2, own, from_west, from_east,
                replies, forecast, part, pay1, pay2, spill,
                states, forcing, vel, rows_of, adds, cell_of, index_v, index_s,
                halo, edge, side, mine_all, beside, beside1, own_f, own_a, sems):
    odd, top, bottom = where_am_i()
    load_x = pltpu.make_async_copy(x, states.at[pl.ds(PAD, ROWS)], sems.at[0])
    load_x.start()
    load_v = pltpu.make_async_copy(vel_in, vel.at[pl.ds(PAD, 2 * K * CL)], sems.at[1])
    load_v.start()
    box = arrived[pl.ds(0, NDEV, stride=MESSAGE), :]
    index_v[...] = (jnp.transpose(box)[2 * CAP : 3 * CAP].astype(i32) >> 7) + PAD
    load_i = pltpu.make_async_copy(index_v, index_s, sems.at[2])
    load_i.start()

    lane = iota((EXT, CW), 1)
    slot = lane & 3
    for n, rows in enumerate(halo_rows(got1, got2, odd)):
        halo[n, : rows.shape[0], :] = rows
    near_slot = iota((CL, CW), 1) & 3
    for kind in range(F + 2):
        side[kind, :CL, :] = jnp.where(near_slot < 2, from_west[kind], from_east[kind])
        side[kind, CL:, :] = jnp.zeros((8, CW), f32)
        mine_all[kind, :CL, :] = own[kind]
        mine_all[kind, CL:, :] = jnp.zeros((8, CW), f32)
        span = slice(kind * K, kind * K + K)
        mine_all[kind, CL : CL + 1, :] = gather_line(halo[0, span, :])
        mine_all[kind, EXT - 1 :, :] = gather_line(halo[2, span, :])
        line = corner_line(arrived, kind, NW, NE)
        side[kind, CL : CL + 1, :] = jnp.where(top, -line, line) if kind in FLIPPED else line
        line = corner_line(arrived, kind, SW, SE)
        side[kind, EXT - 1 :, :] = jnp.where(bottom, 0.0, line)
    base, um, up, vm, vp = parts(side[F], side[F + 1])
    for f in range(F):
        k = kap[f]
        mine = mine_all[f]
        near = side[f]
        e = jnp.where(slot == 1, east(mine), east(near))
        w = jnp.where(slot == 1, west(near), west(mine))
        beside[f] = swapped(near, slot)
        next_near = (
            (base - 4.0 * k) * near
            + (k + um) * e
            + (k + up) * w
            + (k + vm) * north(near)
            + (k + vp) * south(near)
        )
        beside1[f] = swapped(next_near, slot)

    @pl.loop(0, 3 * ROWS // 256)
    def _(i):
        forcing[pl.ds(pl.multiple_of(i * 256, 256) + PAD, 256), :] = jnp.zeros((256, CW), f32)

    first = iota((8, CW), 1) == 0
    last = iota((8, CW), 1) == CW - 1
    row0 = iota((8, CW), 0) == 0
    row7 = iota((8, CW), 0) == 7
    first_k = iota((K, CW), 1) == 0
    last_k = iota((K, CW), 1) == CW - 1
    NORTH, SOUTH = 0, 2
    load_x.wait()
    load_v.wait()

    def line(ref, row, f, base=0):
        return ref[pl.ds(PAD + base + f * K * CL + row, K, stride=CL), :]

    def span(f):
        return slice(f * K, f * K + K)

    for n, at, inner in ((NORTH, CL, CL - 1), (SOUTH, EXT - 1, 0)):
        base, um, up, vm, vp = parts(halo[n, span(F), :], halo[n, span(F + 1), :])
        for f in range(F):
            k = kap[f]
            a = halo[n, span(f), :]
            far = halo[n + 1, span(f), :]
            close = line(states, inner, f)
            to_north, to_south = (far, close) if n == NORTH else (close, far)
            h = spread(side[f, at : at + 1, :])
            b = (
                (base - 4.0 * k) * a
                + (k + um) * east(jnp.where(first_k, h, a))
                + (k + up) * west(jnp.where(last_k, h, a))
                + (k + vm) * to_north
                + (k + vp) * to_south
            )
            if n == SOUTH:
                b = jnp.where(bottom, 0.0, b)
            edge[n // 2, span(f), :] = b

    def around(ref, start, t, north_row, south_row):
        at = start + 8 * t
        a = ref[pl.ds(pl.multiple_of(at, 8), 8), :]
        n = ref[pl.ds(at + 1, 8), :]
        s = ref[pl.ds(at - 1, 8), :]
        if t == TILES - 1:
            n = jnp.where(row7, north_row, n)
        if t == 0:
            s = jnp.where(row0, south_row, s)
        return a, n, s

    def forward(source, target, packed, north_of, south_of):
        @pl.loop(0, K, unroll=UNROLL)
        def _(level):
            turn = 126 - 4 * level
            for t in range(TILES):
                at = pl.multiple_of(PAD + level * CL, 8) + 8 * t
                u = vel[pl.ds(pl.multiple_of(at, 8), 8), :]
                v = vel[pl.ds(pl.multiple_of(at + K * CL, 8), 8), :]
                base, um, up, vm, vp = parts(u, v)
                for f in range(F):
                    k = kap[f]
                    plane = f * K + level
                    start = PAD + source * ROWS + plane * CL
                    a, n, s = around(states, start, t, north_of(plane), south_of(plane))
                    h = pltpu.roll(packed[f, 8 * t : 8 * t + 8, :], turn, axis=1)
                    b = (
                        (base - 4.0 * k) * a
                        + (k + um) * jnp.where(last, h, east(a))
                        + (k + up) * jnp.where(first, h, west(a))
                        + (k + vm) * n
                        + (k + vp) * s
                    )
                    to = PAD + target * ROWS + plane * CL + 8 * t
                    states[pl.ds(pl.multiple_of(to, 8), 8), :] = b

    def halo_row(n):
        return lambda plane: halo[n, pl.ds(plane, 1), :]

    def edge_row(n):
        return lambda plane: edge[n, pl.ds(plane, 1), :]

    forward(0, 1, beside, halo_row(NORTH), halo_row(SOUTH))
    forward(1, 2, beside1, edge_row(0), edge_row(1))
    save = pltpu.make_async_copy(states.at[pl.ds(PAD + 2 * ROWS, ROWS)], forecast, sems.at[3])
    save.start()

    load_i.wait()

    @pl.loop(0, NDEV)
    def _(s):
        for q in range(CAP):
            at = index_s[q, s]
            rows_of[pl.ds(q * NDEV + s, 1), :] = states[pl.ds(at, 1), :]

    lane_s = iota((NDEV, CW), 1)
    cells = box.astype(i32)
    ones = jnp.ones((3 * CW, CW), jnp.bfloat16)
    modelled = jnp.zeros((NDEV, CW), f32)
    for q in range(CAP):
        cut = slice(q * NDEV, (q + 1) * NDEV)
        cell = jnp.broadcast_to(cells[:, 2 * CAP + q : 2 * CAP + q + 1], (NDEV, CW))
        cell_of[cut, :] = cell
        seen = jnp.where(lane_s == cell & (CW - 1), rows_of[cut, :], 0.0)
        seen = jnp.dot(
            jnp.concatenate(thirds(seen), axis=1), ones, preferred_element_type=f32
        )
        modelled = jnp.where(lane_s == q, seen, modelled)
    weight = pltpu.roll(box, CW - CAP, axis=1)
    result = jnp.where(lane_s < CAP, weight * (box - modelled), 0.0)
    replies[...] = jnp.zeros(replies.shape, f32)
    replies[pl.ds(0, NDEV, stride=MESSAGE), :] = result
    for start in range(0, CAP, GROUP):
        for q in range(start, start + GROUP):
            cut = slice(q * NDEV, (q + 1) * NDEV)
            dep = jnp.broadcast_to(result[:, q : q + 1], (NDEV, CW))
            adds[cut, :] = jnp.where(lane_s == cell_of[cut, :] & (CW - 1), dep, 0.0)
        for q in range(start + GROUP - 1, start, -1):
            cut = slice(q * NDEV, (q + 1) * NDEV)
            mine = cell_of[cut, :] >> 7
            acc = adds[cut, :]
            for p in range(start, q):
                other = slice(p * NDEV, (p + 1) * NDEV)
                acc = acc + jnp.where(mine == cell_of[other, :] >> 7, adds[other, :], 0.0)
            adds[cut, :] = acc

    @pl.loop(0, NDEV)
    def _(s):
        for start in range(0, CAP, GROUP):
            ats = [index_s[q, s] for q in range(start, start + GROUP)]
            olds = [forcing[pl.ds(at, 1), :] for at in ats]
            for n in range(GROUP):
                forcing[pl.ds(ats[n], 1), :] = (
                    olds[n] + adds[pl.ds((start + n) * NDEV + s, 1), :]
                )

    own_f[...] = jnp.zeros(own_f.shape, f32)
    own_a[...] = jnp.zeros(own_a.shape, f32)
    group = iota((8, CW), 1) >> 2

    @pl.loop(0, K, unroll=UNROLL)
    def _(level):
        here = group == level
        turn = 4 * level + 2
        for t in range(TILES):
            at = pl.multiple_of(PAD + level * CL, 8) + 8 * t
            u = vel[pl.ds(pl.multiple_of(at, 8), 8), :]
            v, vn, vs = around(vel, PAD + (K + level) * CL, t, 0.0, 0.0)
            base, um, up, _, _ = parts(u, v)
            vm = -jnp.minimum(vs, 0.0)
            vp = jnp.maximum(vn, 0.0)
            cut = slice(8 * t, 8 * t + 8)
            for f in range(F):
                k = kap[f]
                plane = f * K + level
                a, n, s = around(forcing, PAD + 2 * ROWS + plane * CL, t, 0.0, 0.0)
                own_f[f, cut, :] = jnp.where(here, pltpu.roll(a, turn, axis=1), own_f[f, cut, :])
                to = pl.ds(pl.multiple_of(PAD + ROWS + plane * CL + 8 * t, 8), 8)
                more = forcing[to, :]
                own_a[f, cut, :] = jnp.where(here, pltpu.roll(more, turn, axis=1), own_a[f, cut, :])
                b = (
                    (base - 4.0 * k) * a
                    + jnp.where(first, 0.0, west((k + um) * a))
                    + jnp.where(last, 0.0, east((k + up) * a))
                    + (k + vm) * s
                    + (k + vp) * n
                    + more
                )
                forcing[to, :] = b

    for n, at, inner in ((NORTH, CL, CL - 1), (SOUTH, EXT - 1, 0)):
        hu, hv = halo[n, span(F), :], halo[n, span(F + 1), :]
        base, um, up, vm, vp = parts(hu, hv)
        nearest = line(vel, inner, 1)
        push = jnp.maximum(nearest, 0.0) if n == SOUTH else -jnp.minimum(nearest, 0.0)
        on = vp if n == SOUTH else vm
        for f in range(F):
            k = kap[f]
            b = (k + push) * line(forcing, inner, f, 2 * ROWS)
            if n == SOUTH:
                b = jnp.where(bottom, 0.0, b)
            edge[n // 2, span(f), :] = b
            near = (
                (base - 4.0 * k) * b
                + jnp.where(first_k, 0.0, west((k + um) * b))
                + jnp.where(last_k, 0.0, east((k + up) * b))
                + (k + push) * line(forcing, inner, f, ROWS)
            )
            for d, rows in ((0, near), (1, (k + on) * b)):
                to = slice(d * PLANES + f * K, d * PLANES + f * K + K)
                mirrored = reverse_lanes(rows)
                mirrored = -mirrored if f in FLIPPED else mirrored
                if n == NORTH:
                    pay1[to, :] = rows
                    pay2[to, :] = jnp.where(top, mirrored, rows)
                else:
                    pay1[to, :] = jnp.where(odd, rows, pay1[to, :])
                    pay2[to, :] = jnp.where(odd, pay2[to, :], rows)

    base, um, up, vm, vp = parts(side[F], side[F + 1])
    obase, oum, oup, ovm, ovp = parts(mine_all[F], mine_all[F + 1])
    gone = bottom & (iota((EXT, CW), 0) >= CL + 2)
    ends = []
    for f in range(F):
        k = kap[f]
        a = own_f[f]
        oa, ob = (k + oum) * a, (k + oup) * a
        b = jnp.where(slot == 1, east(ob), jnp.where(slot == 2, west(oa), 0.0))
        a = (
            (obase - 4.0 * k) * a
            + jnp.where(slot == 1, west(oa), east(ob))
            + south((k + ovm) * a)
            + north((k + ovp) * a)
        )
        a = jnp.where(gone, 0.0, a) + own_a[f]
        pa = (k + um) * b
        pb = (k + up) * b
        beside1[f] = swapped(jnp.where(slot == 1, pa, pb), slot)
        inner = (
            (base - 4.0 * k) * b
            + south((k + vm) * b)
            + north((k + vp) * b)
            + jnp.where(slot == 1, east((k + oup) * a), west((k + oum) * a))
        )
        outer = jnp.where(slot == 0, east(pb), west(pa))
        beyond = jnp.where((slot == 1) | (slot == 2), inner, outer)
        spill[f] = beyond[:CL]
        ends.append(beyond[CL:])
    post_corners(
        replies,
        [
            corner_rows(ends, 0, 2),
            corner_rows(ends, 0, 1),
            corner_rows(ends, 7, 2),
            corner_rows(ends, 7, 1),
        ],
        bottom,
    )

    def step(level):
        turn = 126 - 4 * level
        for t in range(TILES):
            at = pl.multiple_of(PAD + level * CL, 8) + 8 * t
            u = vel[pl.ds(pl.multiple_of(at, 8), 8), :]
            v, vn, vs = around(
                vel,
                PAD + (K + level) * CL,
                t,
                halo[NORTH, pl.ds((F + 1) * K + level, 1), :],
                halo[SOUTH, pl.ds((F + 1) * K + level, 1), :],
            )
            base, um, up, _, _ = parts(u, v)
            vm = -jnp.minimum(vs, 0.0)
            vp = jnp.maximum(vn, 0.0)
            for f in range(F):
                k = kap[f]
                plane = f * K + level
                start = PAD + ROWS + plane * CL
                a, n, s = around(forcing, start, t, edge_row(0)(plane), edge_row(1)(plane))
                h = pltpu.roll(beside1[f, 8 * t : 8 * t + 8, :], turn, axis=1)
                b = (
                    (base - 4.0 * k) * a
                    + jnp.where(first, h, west((k + um) * a))
                    + jnp.where(last, h, east((k + up) * a))
                    + (k + vm) * s
                    + (k + vp) * n
                    + forcing[pl.ds(pl.multiple_of(PAD + plane * CL + 8 * t, 8), 8), :]
                )
                forcing[pl.ds(pl.multiple_of(PAD + plane * CL + 8 * t, 8), 8), :] = b

    saves = [save]
    for half in range(2):
        pl.loop(half * (K // 2), (half + 1) * (K // 2), unroll=UNROLL)(step)
        for f in range(F):
            at = f * K * CL + half * (K // 2) * CL
            size = K // 2 * CL
            saves.append(
                pltpu.make_async_copy(
                    forcing.at[pl.ds(PAD + at, size)],
                    part.at[pl.ds(at, size)],
                    sems.at[4 + half * F + f],
                )
            )
            saves[-1].start()
    for copy in saves:
        copy.wait()


def finish_kernel(part, from_west, from_east, got1, got2, returned, owner, slots,
                  adjoint, departures, held, sems):
    size = K * CL
    loads, saves = [], []
    for f in range(F):
        cut = pl.ds(f * size, size)
        loads.append(pltpu.make_async_copy(part.at[cut], held.at[cut], sems.at[f]))
        saves.append(pltpu.make_async_copy(held.at[cut], adjoint.at[cut], sems.at[F + f]))
        loads[f].start()

    flat = jnp.transpose(returned[pl.ds(0, NDEV, stride=MESSAGE), :])[:CAP]
    flat = jnp.concatenate(thirds(flat), axis=0)
    dest = iota((NDEV, 128), 0)
    place = iota((CAP, 128), 0).astype(f32)
    for b in range(NBLK):
        hot = (dest == owner[b : b + 1, :]).astype(f32).astype(jnp.bfloat16)
        found = jnp.dot(flat, hot, preferred_element_type=f32)
        found = found[:CAP] + found[CAP : 2 * CAP] + found[2 * CAP :]
        departures[b : b + 1, :] = jnp.sum(
            jnp.where(place == slots[b : b + 1, :], found, 0.0), axis=0, keepdims=True
        )

    odd, top, bottom = where_am_i()
    lane = iota((CL, CW), 1)
    slot = lane & 3
    close = (lane < 2) | (lane >= CW - 2)
    for f in range(F):
        merged = jnp.where(slot < 2, from_east[f], from_west[f])
        loads[f].wait()

        @pl.loop(0, K, unroll=K)
        def _(level):
            more = pltpu.roll(merged, 126 - 4 * level, axis=1)
            at = pl.multiple_of((f * K + level) * CL, CL)
            held[pl.ds(at, CL), :] = held[pl.ds(at, CL), :] + jnp.where(close, more, 0.0)

        north_line = corner_line(returned, f, NE, NW)
        north_line = jnp.where(top, -north_line, north_line) if f in FLIPPED else north_line
        south_line = jnp.where(bottom, 0.0, corner_line(returned, f, SE, SW))
        for d in range(2):
            cut = slice(d * PLANES + f * K, d * PLANES + f * K + K)
            more_up = jnp.where(odd, got2[cut, :], got1[cut, :])
            more_down = jnp.where(odd, got1[cut, :], got2[cut, :])
            if d == 0:
                more_up = more_up + jnp.where(close, spread(north_line), 0.0)
                more_down = more_down + jnp.where(close, spread(south_line), 0.0)
            up = pl.ds(f * size + CL - 1 - d, K, stride=CL)
            held[up, :] = held[up, :] + more_up
            down = pl.ds(f * size + d, K, stride=CL)
            held[down, :] = held[down, :] + more_down
        saves[f].start()
    for copy in saves:
        copy.wait()


def all_to_all(x):
    shape = x.shape
    x = x.reshape(NDEV, 1, MESSAGE * CW)
    x = lax.all_to_all(x, ("lon", "lat"), split_axis=0, concat_axis=0, tiled=True)
    return x.reshape(shape)


def shards(
    background, velocity, diffusivity, obs_value, obs_weight, obs_owner, obs_counts, obs_cell
):
    nlon = lax.axis_size("lon")
    nlat = lax.axis_size("lat")
    both = ("lon", "lat")

    def number(i, j):
        return i * nlat + j

    pairs1 = [(number(i, j), number(i, j ^ 1)) for i in range(nlon) for j in range(nlat)]
    pairs2 = []
    for i in range(nlon):
        for j in range(1, nlat - 1):
            pairs2.append((number(i, j), number(i, j + 1 if j & 1 else j - 1)))
        pairs2.append((number(i, nlat - 1), number(nlon - 1 - i, nlat - 1)))
    eastward = [(i, (i + 1) % nlon) for i in range(nlon)]
    westward = [((i + 1) % nlon, i) for i in range(nlon)]

    def around(x):
        return lax.ppermute(x, "lon", eastward), lax.ppermute(x, "lon", westward)

    x = background.reshape(ROWS, CW)
    vel = velocity.reshape(2 * K * CL, CW)
    own, pay1, pay2 = call(
        edges_kernel,
        [((F + 2, CL, CW), f32)] + [((ALL + PLANES, CW), f32)] * 2,
        [(H, x), (H, vel)],
        "edges",
        scratch=[V((ALL * CL, CW), f32), pltpu.SemaphoreType.DMA((F + 2,))],
    )
    got2 = lax.ppermute(pay2, both, pairs2)
    got1 = lax.ppermute(pay1, both, pairs1)
    from_west, from_east = around(own)

    owner = obs_owner.reshape(NBLK, 128)
    packed, slots = call(
        pack_kernel,
        [((MESSAGE * NDEV, CW), f32), ((NBLK, 128), f32)],
        [
            (S, obs_counts),
            (V, obs_value.reshape(NBLK, 128)),
            (V, obs_weight.reshape(NBLK, 128)),
            (V, owner),
            (V, obs_cell.reshape(NBLK, 128)),
            (V, own),
        ],
        "pack",
    )
    arrived = all_to_all(packed)
    padded = 3 * ROWS + 2 * PAD
    replies, forecast, part, pay1, pay2, spill = call(
        core_kernel,
        [
            ((MESSAGE * NDEV, CW), f32),
            ((ROWS, CW), f32, H),
            ((ROWS, CW), f32, H),
            ((2 * PLANES, CW), f32),
            ((2 * PLANES, CW), f32),
            ((F, CL, CW), f32),
        ],
        [
            (S, diffusivity),
            (V, arrived),
            (H, x),
            (H, vel),
            (V, got1),
            (V, got2),
            (V, own),
            (V, from_west),
            (V, from_east),
        ],
        "core",
        scratch=[
            V((padded, CW), f32),
            V((padded, CW), f32),
            V((2 * K * CL + 2 * PAD, CW), f32),
            V((CAP * NDEV, CW), f32),
            V((CAP * NDEV, CW), f32),
            V((CAP * NDEV, CW), i32),
            V((CAP, 128), i32),
            S((CAP, 128), i32),
            V((4, ALL, CW), f32),
            V((2, PLANES, CW), f32),
            V((F + 2, EXT, CW), f32),
            V((F + 2, EXT, CW), f32),
            V((F, EXT, CW), f32),
            V((F, EXT, CW), f32),
            V((F, EXT, CW), f32),
            V((F, EXT, CW), f32),
            pltpu.SemaphoreType.DMA((4 + 2 * F,)),
        ],
    )
    back2 = lax.ppermute(pay2, both, pairs2)
    back1 = lax.ppermute(pay1, both, pairs1)
    spill_west, spill_east = around(spill)
    returned = all_to_all(replies)
    adjoint, found = call(
        finish_kernel,
        [((ROWS, CW), f32, H), ((NBLK, 128), f32)],
        [
            (H, part),
            (V, spill_west),
            (V, spill_east),
            (V, back1),
            (V, back2),
            (V, returned),
            (V, owner),
            (V, slots),
        ],
        "finish",
        scratch=[V((ROWS, CW), f32), pltpu.SemaphoreType.DMA((2 * F,))],
    )
    shape = (F, K, CL, CW)
    return forecast.reshape(shape), adjoint.reshape(shape), found.reshape(-1)


def solution(mesh):
    in_specs = (
        P(None, None, "lat", "lon"),
        P(None, None, "lat", "lon"),
        P(),
        P(("lon", "lat")),
        P(("lon", "lat")),
        P(("lon", "lat"), None),
        P(("lon", "lat"), None),
        P(("lon", "lat")),
    )
    out_specs = (P(None, None, "lat", "lon"), P(None, None, "lat", "lon"), P(("lon", "lat")))
    return jax.shard_map(shards, mesh=mesh, in_specs=in_specs, out_specs=out_specs, check_vma=False)
```

```python
import jax
import jax.numpy as jnp
from jax import lax
from jax.experimental import pallas as pl
from jax.experimental.pallas import tpu as pltpu
from jax.sharding import PartitionSpec as P


STEPS = 2
F = 5
K = 32
CL = 32
CW = 128
PLANES = F * K
ALL = PLANES + 2 * K
EXT = 40
ROWS = PLANES * CL
NBLK = 8
NDEV = 128
CAP = 16
MIB = 1 << 20
f32 = jnp.float32
i32 = jnp.int32


V = pltpu.VMEM
S = pltpu.SMEM
H = pltpu.HBM


def iota(shape, dim):
    return lax.broadcasted_iota(i32, shape, dim)


def call(body, outs, ins, name, scratch=(), vmem=53, flops=10**6, nbytes=10**6):
    return pl.pallas_call(
        body,
        out_shape=[jax.ShapeDtypeStruct(shape, dtype) for shape, dtype, *_ in outs],
        in_specs=[pl.BlockSpec(memory_space=space) for space, _ in ins],
        out_specs=[pl.BlockSpec(memory_space=out[2] if len(out) > 2 else V) for out in outs],
        scratch_shapes=list(scratch),
        compiler_params=pltpu.CompilerParams(vmem_limit_bytes=vmem * MIB),
        cost_estimate=pl.CostEstimate(flops=flops, bytes_accessed=nbytes, transcendentals=0),
        name=name,
    )(*[x for _, x in ins])


def reverse_lanes(x):
    return jnp.take_along_axis(x, 127 - iota(x.shape, 1), axis=1)


def fold_sign(planes):
    kind = iota((planes, CW), 0) // K
    return jnp.where((kind == 2) | (kind == 3) | (kind >= F), -1.0, 1.0).astype(f32)


def where_am_i():
    at = lax.axis_index("lat")
    return at & 1 == 1, at == lax.axis_size("lat") - 1, at == 0


def partners():
    i, j = lax.axis_index("lon"), lax.axis_index("lat")
    n, m = lax.axis_size("lon"), lax.axis_size("lat")
    top = j == m - 1
    to_east, to_west = lax.rem(i + 1, n), lax.rem(i + n - 1, n)
    north_of, south_of = jnp.minimum(j + 1, m - 1), jnp.maximum(j - 1, 0)
    return (
        jnp.where(top, lax.rem(2 * n - 2 - i, n), to_east) * m + north_of,
        jnp.where(top, lax.rem(n - i, n), to_west) * m + north_of,
        to_east * m + south_of,
        to_west * m + south_of,
    )


def corner_rows(blocks, line, place):
    lane = iota((8, CW), 1)
    row = jnp.zeros((8, CW), f32)
    for f in range(F - 1):
        row = jnp.where(lane & 3 == f, pltpu.roll(blocks[f], (f - place) % CW, axis=1), row)
    picked = (4 * (lane - TAIL) + place) & (CW - 1)
    tail = jnp.take_along_axis(blocks[F - 1], picked, axis=1)
    return tail[line : line + 1], row[line : line + 1]


def post_corners(pay, rows, bottom):
    tail = iota((1, CW), 1) >= TAIL
    for n, at in enumerate(partners()):
        @pl.when(jnp.logical_not(bottom) if n >= 2 else at >= 0)
        def _(n=n, at=at):
            to = pl.ds(MESSAGE * at, 1)
            pay[to, :] = jnp.where(tail, rows[n][0], pay[to, :])
            pay[pl.ds(MESSAGE * at + 1, 1), :] = rows[n][1]


def corner_line(got, f, first, second):
    lane = iota((8, CW), 1)
    ats = partners()
    line = jnp.zeros((8, CW), f32)
    for place, n in ((1, first), (2, second)):
        row = got[pl.ds(MESSAGE * ats[n] + (0 if f == F - 1 else 1), 1), :]
        row = jnp.broadcast_to(row, (8, CW))
        if f == F - 1:
            moved = jnp.take_along_axis(row, TAIL + (lane >> 2), axis=1)
        else:
            moved = pltpu.roll(row, (place - f) % CW, axis=1)
        line = jnp.where(lane & 3 == place, moved, line)
    return line[:1]


NE, NW, SE, SW = range(4)
MESSAGE = 2
TAIL = CW - K
FLIPPED = (2, 3)


def thirds(x):
    pieces = []
    for _ in range(3):
        piece = x.astype(jnp.bfloat16)
        pieces.append(piece)
        x = x - piece.astype(f32)
    return pieces


def edges_kernel(x, vel, own, pay1, pay2, held, sems):
    odd, top, _ = where_am_i()
    copies = []
    for kind in range(F + 2):
        ref, plane = (x, kind * K) if kind < F else (vel, (kind - F) * K)
        copies.append(
            pltpu.make_async_copy(
                ref.at[pl.ds(plane * CL, K * CL)],
                held.at[pl.ds(kind * K * CL, K * CL)],
                sems.at[kind],
            )
        )
    for copy in copies:
        copy.start()
    group = iota((CL, CW), 1) >> 2
    for kind in range(F + 2):
        copies[kind].wait()
        for d in range(2 if kind < F else 1):
            low = held[pl.ds(kind * K * CL + d, K, stride=CL), :]
            high = held[pl.ds(kind * K * CL + CL - 1 - d, K, stride=CL), :]
            to = slice(d * ALL + kind * K, d * ALL + kind * K + K)
            pay1[to, :] = jnp.where(odd, low, high)
            pay2[to, :] = jnp.where(odd, high, low)

        def step(level, packed):
            rows = held[pl.ds(pl.multiple_of((kind * K + level) * CL, CL), CL), :]
            moved = pltpu.roll(rows, 4 * level + 2, axis=1)
            return jnp.where(group == level, moved, packed)

        own[kind] = lax.fori_loop(0, K, step, jnp.zeros((CL, CW), f32), unroll=True)

    @pl.when(top)
    def _():
        pay2[:ALL, :] = fold_sign(ALL) * reverse_lanes(pay2[:ALL, :])
        pay2[ALL:, :] = fold_sign(PLANES) * reverse_lanes(pay2[ALL:, :])


def halo_rows(got1, got2, odd):
    near, far = slice(0, ALL), slice(ALL, ALL + PLANES)
    norths = [jnp.where(odd, got2[cut, :], got1[cut, :]) for cut in (near, far)]
    souths = [jnp.where(odd, got1[cut, :], got2[cut, :]) for cut in (near, far)]
    return norths + souths


def spread(line):
    level, lane = iota((K, CW), 0), iota((K, CW), 1)
    return jnp.take_along_axis(
        jnp.broadcast_to(line, (K, CW)), (lane + 4 * level + 2) & (CW - 1), axis=1
    )


def gather_line(rows):
    level, lane = iota((K, CW), 0), iota((K, CW), 1)
    moved = jnp.take_along_axis(rows, (lane - 4 * level - 2) & (CW - 1), axis=1)
    return jnp.sum(jnp.where(lane >> 2 == level, moved, 0.0), axis=0, keepdims=True)


def north(x):
    return pltpu.roll(x, EXT - 1, axis=0)


def south(x):
    return pltpu.roll(x, 1, axis=0)


def east(x):
    return pltpu.roll(x, CW - 1, axis=1)


def west(x):
    return pltpu.roll(x, 1, axis=1)


def swapped(x, slot):
    return jnp.where(slot == 1, east(x), jnp.where(slot == 2, west(x), x))


def parts(u, v):
    return (
        1.0 - jnp.abs(u) - jnp.abs(v),
        -jnp.minimum(u, 0.0),
        jnp.maximum(u, 0.0),
        -jnp.minimum(v, 0.0),
        jnp.maximum(v, 0.0),
    )


def pack_kernel(counts, value, weight, owner, cell, own, pay, slots):
    dest = iota((NDEV, 128), 0)
    lane = iota((1, 128), 1)
    before = (iota((128, 128), 0) < iota((128, 128), 1)).astype(f32).astype(jnp.bfloat16)
    ones = jnp.ones((128, 128), jnp.bfloat16)
    carry = jnp.zeros((NDEV, 128), f32)
    total = jnp.zeros((NDEV, 128), f32)
    place = iota((CAP, 128), 0).astype(f32)
    for b in range(NBLK):
        live = lane < counts[0, b]
        who = jnp.where(live, owner[b : b + 1, :], -1)
        hot = (dest == who).astype(f32)
        hot16 = hot.astype(jnp.bfloat16)
        earlier = carry + jnp.dot(hot16, before, preferred_element_type=f32)
        carry = carry + jnp.dot(hot16, ones, preferred_element_type=f32)
        slot = jnp.sum(hot * earlier, axis=0, keepdims=True)
        slot = jnp.where(live, slot, -1.0)
        slots[b : b + 1, :] = slot
        code = (cell[b : b + 1, :] + (b % (STEPS + 1)) * (ROWS * CW)).astype(f32)
        here = place == slot
        fields = [
            jnp.where(here, data, 0.0) for data in (value[b : b + 1, :], weight[b : b + 1, :], code)
        ]
        fields.append(jnp.zeros((128 - 3 * CAP, 128), f32))
        total = total + lax.dot_general(
            jnp.concatenate([hot16] * 3, axis=1),
            jnp.concatenate(thirds(jnp.concatenate(fields, axis=0)), axis=1),
            (((1,), (1,)), ((), ())),
            preferred_element_type=f32,
        )
    pay[...] = jnp.zeros(pay.shape, f32)
    pay[pl.ds(0, NDEV, stride=MESSAGE), :] = total
    low = [own[f, :8, :] for f in range(F)]
    high = [own[f, CL - 8 :, :] for f in range(F)]
    _, _, bottom = where_am_i()
    post_corners(
        pay,
        [
            corner_rows(high, 7, 1),
            corner_rows(high, 7, 2),
            corner_rows(low, 0, 1),
            corner_rows(low, 0, 2),
        ],
        bottom,
    )


PAD = 8
GROUP = 8
UNROLL = 8
TILES = CL // 8


def core_kernel(kap, arrived, x, vel_in, got1, got2, own, from_west, from_east,
                replies, forecast, part, pay1, pay2, spill,
                states, forcing, vel, rows_of, adds, cell_of, index_v, index_s,
                halo, edge, side, mine_all, beside, beside1, own_f, own_a, sems):
    odd, top, bottom = where_am_i()
    load_x = pltpu.make_async_copy(x, states.at[pl.ds(PAD, ROWS)], sems.at[0])
    load_x.start()
    load_v = pltpu.make_async_copy(vel_in, vel.at[pl.ds(PAD, 2 * K * CL)], sems.at[1])
    load_v.start()
    box = arrived[pl.ds(0, NDEV, stride=MESSAGE), :]
    index_v[...] = (jnp.transpose(box)[2 * CAP : 3 * CAP].astype(i32) >> 7) + PAD
    load_i = pltpu.make_async_copy(index_v, index_s, sems.at[2])
    load_i.start()

    lane = iota((EXT, CW), 1)
    slot = lane & 3
    for n, rows in enumerate(halo_rows(got1, got2, odd)):
        halo[n, : rows.shape[0], :] = rows
    near_slot = iota((CL, CW), 1) & 3
    for kind in range(F + 2):
        side[kind, :CL, :] = jnp.where(near_slot < 2, from_west[kind], from_east[kind])
        side[kind, CL:, :] = jnp.zeros((8, CW), f32)
        mine_all[kind, :CL, :] = own[kind]
        mine_all[kind, CL:, :] = jnp.zeros((8, CW), f32)
        span = slice(kind * K, kind * K + K)
        mine_all[kind, CL : CL + 1, :] = gather_line(halo[0, span, :])
        mine_all[kind, EXT - 1 :, :] = gather_line(halo[2, span, :])
        if kind < F:
            line = corner_line(arrived, kind, NW, NE)
            side[kind, CL : CL + 1, :] = jnp.where(top, -line, line) if kind in FLIPPED else line
            line = corner_line(arrived, kind, SW, SE)
            side[kind, EXT - 1 :, :] = jnp.where(bottom, 0.0, line)
    base, um, up, vm, vp = parts(side[F], side[F + 1])
    for f in range(F):
        k = kap[f]
        mine = mine_all[f]
        near = side[f]
        e = jnp.where(slot == 1, east(mine), east(near))
        w = jnp.where(slot == 1, west(near), west(mine))
        beside[f] = swapped(near, slot)
        next_near = (
            (base - 4.0 * k) * near
            + (k + um) * e
            + (k + up) * w
            + (k + vm) * north(near)
            + (k + vp) * south(near)
        )
        beside1[f] = swapped(next_near, slot)

    @pl.loop(0, 3 * ROWS // 256)
    def _(i):
        forcing[pl.ds(pl.multiple_of(i * 256, 256) + PAD, 256), :] = jnp.zeros((256, CW), f32)

    first = iota((8, CW), 1) == 0
    last = iota((8, CW), 1) == CW - 1
    row0 = iota((8, CW), 0) == 0
    row7 = iota((8, CW), 0) == 7
    first_k = iota((K, CW), 1) == 0
    last_k = iota((K, CW), 1) == CW - 1
    NORTH, SOUTH = 0, 2
    load_x.wait()
    load_v.wait()

    def line(ref, row, f, base=0):
        return ref[pl.ds(PAD + base + f * K * CL + row, K, stride=CL), :]

    def span(f):
        return slice(f * K, f * K + K)

    for n, at, inner in ((NORTH, CL, CL - 1), (SOUTH, EXT - 1, 0)):
        base, um, up, vm, vp = parts(halo[n, span(F), :], halo[n, span(F + 1), :])
        for f in range(F):
            k = kap[f]
            a = halo[n, span(f), :]
            far = halo[n + 1, span(f), :]
            close = line(states, inner, f)
            to_north, to_south = (far, close) if n == NORTH else (close, far)
            h = spread(side[f, at : at + 1, :])
            b = (
                (base - 4.0 * k) * a
                + (k + um) * east(jnp.where(first_k, h, a))
                + (k + up) * west(jnp.where(last_k, h, a))
                + (k + vm) * to_north
                + (k + vp) * to_south
            )
            if n == SOUTH:
                b = jnp.where(bottom, 0.0, b)
            edge[n // 2, span(f), :] = b

    def around(ref, start, t, north_row, south_row):
        at = start + 8 * t
        a = ref[pl.ds(pl.multiple_of(at, 8), 8), :]
        n = ref[pl.ds(at + 1, 8), :]
        s = ref[pl.ds(at - 1, 8), :]
        if t == TILES - 1:
            n = jnp.where(row7, north_row, n)
        if t == 0:
            s = jnp.where(row0, south_row, s)
        return a, n, s

    def forward(source, target, packed, north_of, south_of):
        @pl.loop(0, K, unroll=UNROLL)
        def _(level):
            turn = 126 - 4 * level
            for t in range(TILES):
                at = pl.multiple_of(PAD + level * CL, 8) + 8 * t
                u = vel[pl.ds(pl.multiple_of(at, 8), 8), :]
                v = vel[pl.ds(pl.multiple_of(at + K * CL, 8), 8), :]
                base, um, up, vm, vp = parts(u, v)
                for f in range(F):
                    k = kap[f]
                    plane = f * K + level
                    start = PAD + source * ROWS + plane * CL
                    a, n, s = around(states, start, t, north_of(plane), south_of(plane))
                    h = pltpu.roll(packed[f, 8 * t : 8 * t + 8, :], turn, axis=1)
                    b = (
                        (base - 4.0 * k) * a
                        + (k + um) * jnp.where(last, h, east(a))
                        + (k + up) * jnp.where(first, h, west(a))
                        + (k + vm) * n
                        + (k + vp) * s
                    )
                    to = PAD + target * ROWS + plane * CL + 8 * t
                    states[pl.ds(pl.multiple_of(to, 8), 8), :] = b

    def halo_row(n):
        return lambda plane: halo[n, pl.ds(plane, 1), :]

    def edge_row(n):
        return lambda plane: edge[n, pl.ds(plane, 1), :]

    forward(0, 1, beside, halo_row(NORTH), halo_row(SOUTH))
    forward(1, 2, beside1, edge_row(0), edge_row(1))
    save = pltpu.make_async_copy(states.at[pl.ds(PAD + 2 * ROWS, ROWS)], forecast, sems.at[3])
    save.start()

    load_i.wait()

    @pl.loop(0, NDEV, unroll=4)
    def _(s):
        for q in range(CAP):
            at = index_s[q, s]
            rows_of[pl.ds(q * NDEV + s, 1), :] = states[pl.ds(at, 1), :]

    lane_s = iota((NDEV, CW), 1)
    cells = box.astype(i32)
    ones = jnp.ones((3 * CW, CW), jnp.bfloat16)
    modelled = jnp.zeros((NDEV, CW), f32)
    for q in range(CAP):
        cut = slice(q * NDEV, (q + 1) * NDEV)
        cell = jnp.broadcast_to(cells[:, 2 * CAP + q : 2 * CAP + q + 1], (NDEV, CW))
        cell_of[cut, :] = cell
        seen = jnp.where(lane_s == cell & (CW - 1), rows_of[cut, :], 0.0)
        seen = jnp.dot(
            jnp.concatenate(thirds(seen), axis=1), ones, preferred_element_type=f32
        )
        modelled = jnp.where(lane_s == q, seen, modelled)
    weight = pltpu.roll(box, CW - CAP, axis=1)
    result = jnp.where(lane_s < CAP, weight * (box - modelled), 0.0)
    replies[...] = jnp.zeros(replies.shape, f32)
    replies[pl.ds(0, NDEV, stride=MESSAGE), :] = result
    for start in range(0, CAP, GROUP):
        for q in range(start, start + GROUP):
            cut = slice(q * NDEV, (q + 1) * NDEV)
            dep = jnp.broadcast_to(result[:, q : q + 1], (NDEV, CW))
            adds[cut, :] = jnp.where(lane_s == cell_of[cut, :] & (CW - 1), dep, 0.0)
        for q in range(start + GROUP - 1, start, -1):
            cut = slice(q * NDEV, (q + 1) * NDEV)
            mine = cell_of[cut, :] >> 7
            acc = adds[cut, :]
            for p in range(start, q):
                other = slice(p * NDEV, (p + 1) * NDEV)
                acc = acc + jnp.where(mine == cell_of[other, :] >> 7, adds[other, :], 0.0)
            adds[cut, :] = acc

    @pl.loop(0, NDEV, unroll=4)
    def _(s):
        for start in range(0, CAP, GROUP):
            ats = [index_s[q, s] for q in range(start, start + GROUP)]
            olds = [forcing[pl.ds(at, 1), :] for at in ats]
            for n in range(GROUP):
                forcing[pl.ds(ats[n], 1), :] = (
                    olds[n] + adds[pl.ds((start + n) * NDEV + s, 1), :]
                )

    own_f[...] = jnp.zeros(own_f.shape, f32)
    own_a[...] = jnp.zeros(own_a.shape, f32)
    group = iota((8, CW), 1) >> 2

    @pl.loop(0, K, unroll=UNROLL)
    def _(level):
        here = group == level
        turn = 4 * level + 2
        for t in range(TILES):
            at = pl.multiple_of(PAD + level * CL, 8) + 8 * t
            u = vel[pl.ds(pl.multiple_of(at, 8), 8), :]
            v, vn, vs = around(vel, PAD + (K + level) * CL, t, 0.0, 0.0)
            base, um, up, _, _ = parts(u, v)
            vm = -jnp.minimum(vs, 0.0)
            vp = jnp.maximum(vn, 0.0)
            cut = slice(8 * t, 8 * t + 8)
            for f in range(F):
                k = kap[f]
                plane = f * K + level
                a, n, s = around(forcing, PAD + 2 * ROWS + plane * CL, t, 0.0, 0.0)
                own_f[f, cut, :] = jnp.where(here, pltpu.roll(a, turn, axis=1), own_f[f, cut, :])
                to = pl.ds(pl.multiple_of(PAD + ROWS + plane * CL + 8 * t, 8), 8)
                more = forcing[to, :]
                own_a[f, cut, :] = jnp.where(here, pltpu.roll(more, turn, axis=1), own_a[f, cut, :])
                b = (
                    (base - 4.0 * k) * a
                    + jnp.where(first, 0.0, west((k + um) * a))
                    + jnp.where(last, 0.0, east((k + up) * a))
                    + (k + vm) * s
                    + (k + vp) * n
                    + more
                )
                forcing[to, :] = b

    for n, at, inner in ((NORTH, CL, CL - 1), (SOUTH, EXT - 1, 0)):
        hu, hv = halo[n, span(F), :], halo[n, span(F + 1), :]
        base, um, up, vm, vp = parts(hu, hv)
        nearest = line(vel, inner, 1)
        push = jnp.maximum(nearest, 0.0) if n == SOUTH else -jnp.minimum(nearest, 0.0)
        on = vp if n == SOUTH else vm
        for f in range(F):
            k = kap[f]
            b = (k + push) * line(forcing, inner, f, 2 * ROWS)
            if n == SOUTH:
                b = jnp.where(bottom, 0.0, b)
            edge[n // 2, span(f), :] = b
            near = (
                (base - 4.0 * k) * b
                + jnp.where(first_k, 0.0, west((k + um) * b))
                + jnp.where(last_k, 0.0, east((k + up) * b))
                + (k + push) * line(forcing, inner, f, ROWS)
            )
            for d, rows in ((0, near), (1, (k + on) * b)):
                to = slice(d * PLANES + f * K, d * PLANES + f * K + K)
                mirrored = reverse_lanes(rows)
                mirrored = -mirrored if f in FLIPPED else mirrored
                if n == NORTH:
                    pay1[to, :] = rows
                    pay2[to, :] = jnp.where(top, mirrored, rows)
                else:
                    pay1[to, :] = jnp.where(odd, rows, pay1[to, :])
                    pay2[to, :] = jnp.where(odd, pay2[to, :], rows)

    base, um, up, vm, vp = parts(side[F], side[F + 1])
    obase, oum, oup, ovm, ovp = parts(mine_all[F], mine_all[F + 1])
    gone = bottom & (iota((EXT, CW), 0) >= CL + 2)
    ends = []
    for f in range(F):
        k = kap[f]
        a = own_f[f]
        oa, ob = (k + oum) * a, (k + oup) * a
        b = jnp.where(slot == 1, east(ob), jnp.where(slot == 2, west(oa), 0.0))
        a = (
            (obase - 4.0 * k) * a
            + jnp.where(slot == 1, west(oa), east(ob))
            + south((k + ovm) * a)
            + north((k + ovp) * a)
        )
        a = jnp.where(gone, 0.0, a) + own_a[f]
        pa = (k + um) * b
        pb = (k + up) * b
        beside1[f] = swapped(jnp.where(slot == 1, pa, pb), slot)
        inner = (
            (base - 4.0 * k) * b
            + south((k + vm) * b)
            + north((k + vp) * b)
            + jnp.where(slot == 1, east((k + oup) * a), west((k + oum) * a))
        )
        outer = jnp.where(slot == 0, east(pb), west(pa))
        beyond = jnp.where((slot == 1) | (slot == 2), inner, outer)
        spill[f] = beyond[:CL]
        ends.append(beyond[CL:])
    post_corners(
        replies,
        [
            corner_rows(ends, 0, 2),
            corner_rows(ends, 0, 1),
            corner_rows(ends, 7, 2),
            corner_rows(ends, 7, 1),
        ],
        bottom,
    )

    def step(level):
        turn = 126 - 4 * level
        for t in range(TILES):
            at = pl.multiple_of(PAD + level * CL, 8) + 8 * t
            u = vel[pl.ds(pl.multiple_of(at, 8), 8), :]
            v, vn, vs = around(
                vel,
                PAD + (K + level) * CL,
                t,
                halo[NORTH, pl.ds((F + 1) * K + level, 1), :],
                halo[SOUTH, pl.ds((F + 1) * K + level, 1), :],
            )
            base, um, up, _, _ = parts(u, v)
            vm = -jnp.minimum(vs, 0.0)
            vp = jnp.maximum(vn, 0.0)
            for f in range(F):
                k = kap[f]
                plane = f * K + level
                start = PAD + ROWS + plane * CL
                a, n, s = around(forcing, start, t, edge_row(0)(plane), edge_row(1)(plane))
                h = pltpu.roll(beside1[f, 8 * t : 8 * t + 8, :], turn, axis=1)
                b = (
                    (base - 4.0 * k) * a
                    + jnp.where(first, h, west((k + um) * a))
                    + jnp.where(last, h, east((k + up) * a))
                    + (k + vm) * s
                    + (k + vp) * n
                    + forcing[pl.ds(pl.multiple_of(PAD + plane * CL + 8 * t, 8), 8), :]
                )
                forcing[pl.ds(pl.multiple_of(PAD + plane * CL + 8 * t, 8), 8), :] = b

    saves = [save]
    for half in range(2):
        pl.loop(half * (K // 2), (half + 1) * (K // 2), unroll=UNROLL)(step)
        for f in range(F):
            at = f * K * CL + half * (K // 2) * CL
            size = K // 2 * CL
            saves.append(
                pltpu.make_async_copy(
                    forcing.at[pl.ds(PAD + at, size)],
                    part.at[pl.ds(at, size)],
                    sems.at[4 + half * F + f],
                )
            )
            saves[-1].start()
    for copy in saves:
        copy.wait()


def finish_kernel(part, from_west, from_east, got1, got2, returned, owner, slots,
                  adjoint, departures, held, sems):
    size = K * CL
    loads, saves = [], []
    for f in range(F):
        cut = pl.ds(f * size, size)
        loads.append(pltpu.make_async_copy(part.at[cut], held.at[cut], sems.at[f]))
        saves.append(pltpu.make_async_copy(held.at[cut], adjoint.at[cut], sems.at[F + f]))
        loads[f].start()

    flat = jnp.transpose(returned[pl.ds(0, NDEV, stride=MESSAGE), :])[:CAP]
    flat = jnp.concatenate(thirds(flat), axis=0)
    dest = iota((NDEV, 128), 0)
    place = iota((CAP, 128), 0).astype(f32)
    for b in range(NBLK):
        hot = (dest == owner[b : b + 1, :]).astype(f32).astype(jnp.bfloat16)
        found = jnp.dot(flat, hot, preferred_element_type=f32)
        found = found[:CAP] + found[CAP : 2 * CAP] + found[2 * CAP :]
        departures[b : b + 1, :] = jnp.sum(
            jnp.where(place == slots[b : b + 1, :], found, 0.0), axis=0, keepdims=True
        )

    odd, top, bottom = where_am_i()
    lane = iota((CL, CW), 1)
    slot = lane & 3
    close = (lane < 2) | (lane >= CW - 2)
    for f in range(F):
        merged = jnp.where(slot < 2, from_east[f], from_west[f])
        loads[f].wait()

        @pl.loop(0, K, unroll=K)
        def _(level):
            more = pltpu.roll(merged, 126 - 4 * level, axis=1)
            at = pl.multiple_of((f * K + level) * CL, CL)
            held[pl.ds(at, CL), :] = held[pl.ds(at, CL), :] + jnp.where(close, more, 0.0)

        north_line = corner_line(returned, f, NE, NW)
        north_line = jnp.where(top, -north_line, north_line) if f in FLIPPED else north_line
        south_line = jnp.where(bottom, 0.0, corner_line(returned, f, SE, SW))
        for d in range(2):
            cut = slice(d * PLANES + f * K, d * PLANES + f * K + K)
            more_up = jnp.where(odd, got2[cut, :], got1[cut, :])
            more_down = jnp.where(odd, got1[cut, :], got2[cut, :])
            if d == 0:
                more_up = more_up + jnp.where(close, spread(north_line), 0.0)
                more_down = more_down + jnp.where(close, spread(south_line), 0.0)
            up = pl.ds(f * size + CL - 1 - d, K, stride=CL)
            held[up, :] = held[up, :] + more_up
            down = pl.ds(f * size + d, K, stride=CL)
            held[down, :] = held[down, :] + more_down
        saves[f].start()
    for copy in saves:
        copy.wait()


def all_to_all(x):
    shape = x.shape
    x = x.reshape(NDEV, 1, MESSAGE * CW)
    x = lax.all_to_all(x, ("lon", "lat"), split_axis=0, concat_axis=0, tiled=True)
    return x.reshape(shape)


def shards(
    background, velocity, diffusivity, obs_value, obs_weight, obs_owner, obs_counts, obs_cell
):
    nlon = lax.axis_size("lon")
    nlat = lax.axis_size("lat")
    both = ("lon", "lat")

    def number(i, j):
        return i * nlat + j

    pairs1 = [(number(i, j), number(i, j ^ 1)) for i in range(nlon) for j in range(nlat)]
    pairs2 = []
    for i in range(nlon):
        for j in range(1, nlat - 1):
            pairs2.append((number(i, j), number(i, j + 1 if j & 1 else j - 1)))
        pairs2.append((number(i, nlat - 1), number(nlon - 1 - i, nlat - 1)))
    eastward = [(i, (i + 1) % nlon) for i in range(nlon)]
    westward = [((i + 1) % nlon, i) for i in range(nlon)]

    def around(x):
        return lax.ppermute(x, "lon", eastward), lax.ppermute(x, "lon", westward)

    x = background.reshape(ROWS, CW)
    vel = velocity.reshape(2 * K * CL, CW)
    own, pay1, pay2 = call(
        edges_kernel,
        [((F + 2, CL, CW), f32)] + [((ALL + PLANES, CW), f32)] * 2,
        [(H, x), (H, vel)],
        "edges",
        scratch=[V((ALL * CL, CW), f32), pltpu.SemaphoreType.DMA((F + 2,))],
    )
    got2 = lax.ppermute(pay2, both, pairs2)
    from_west, from_east = around(own)

    owner = obs_owner.reshape(NBLK, 128)
    packed, slots = call(
        pack_kernel,
        [((MESSAGE * NDEV, CW), f32), ((NBLK, 128), f32)],
        [
            (S, obs_counts),
            (V, obs_value.reshape(NBLK, 128)),
            (V, obs_weight.reshape(NBLK, 128)),
            (V, owner),
            (V, obs_cell.reshape(NBLK, 128)),
            (V, own),
        ],
        "pack",
    )
    pay1, packed = lax.optimization_barrier((pay1, packed))
    got1 = lax.ppermute(pay1, both, pairs1)
    arrived = all_to_all(packed)
    padded = 3 * ROWS + 2 * PAD
    replies, forecast, part, pay1, pay2, spill = call(
        core_kernel,
        [
            ((MESSAGE * NDEV, CW), f32),
            ((ROWS, CW), f32, H),
            ((ROWS, CW), f32, H),
            ((2 * PLANES, CW), f32),
            ((2 * PLANES, CW), f32),
            ((F, CL, CW), f32),
        ],
        [
            (S, diffusivity),
            (V, arrived),
            (H, x),
            (H, vel),
            (V, got1),
            (V, got2),
            (V, own),
            (V, from_west),
            (V, from_east),
        ],
        "core",
        scratch=[
            V((padded, CW), f32),
            V((padded, CW), f32),
            V((2 * K * CL + 2 * PAD, CW), f32),
            V((CAP * NDEV, CW), f32),
            V((CAP * NDEV, CW), f32),
            V((CAP * NDEV, CW), i32),
            V((CAP, 128), i32),
            S((CAP, 128), i32),
            V((4, ALL, CW), f32),
            V((2, PLANES, CW), f32),
            V((F + 2, EXT, CW), f32),
            V((F + 2, EXT, CW), f32),
            V((F, EXT, CW), f32),
            V((F, EXT, CW), f32),
            V((F, EXT, CW), f32),
            V((F, EXT, CW), f32),
            pltpu.SemaphoreType.DMA((4 + 2 * F,)),
        ],
    )
    back2 = lax.ppermute(pay2, both, pairs2)
    back1 = lax.ppermute(pay1, both, pairs1)
    spill_west, spill_east = around(spill)
    returned = all_to_all(replies)
    adjoint, found = call(
        finish_kernel,
        [((ROWS, CW), f32, H), ((NBLK, 128), f32)],
        [
            (H, part),
            (V, spill_west),
            (V, spill_east),
            (V, back1),
            (V, back2),
            (V, returned),
            (V, owner),
            (V, slots),
        ],
        "finish",
        scratch=[V((ROWS, CW), f32), pltpu.SemaphoreType.DMA((2 * F,))],
    )
    shape = (F, K, CL, CW)
    return forecast.reshape(shape), adjoint.reshape(shape), found.reshape(-1)


def solution(mesh):
    in_specs = (
        P(None, None, "lat", "lon"),
        P(None, None, "lat", "lon"),
        P(),
        P(("lon", "lat")),
        P(("lon", "lat")),
        P(("lon", "lat"), None),
        P(("lon", "lat"), None),
        P(("lon", "lat")),
    )
    out_specs = (P(None, None, "lat", "lon"), P(None, None, "lat", "lon"), P(("lon", "lat")))
    return jax.shard_map(shards, mesh=mesh, in_specs=in_specs, out_specs=out_specs, check_vma=False)
```

```python
import jax
import jax.numpy as jnp
from jax import lax
from jax.experimental import pallas as pl
from jax.experimental.pallas import tpu as pltpu
from jax.sharding import PartitionSpec as P


STEPS = 2
F = 5
K = 32
CL = 32
CW = 128
PLANES = F * K
ALL = PLANES + 2 * K
EXT = 40
ROWS = PLANES * CL
NBLK = 8
NDEV = 128
CAP = 16
MIB = 1 << 20
f32 = jnp.float32
i32 = jnp.int32


V = pltpu.VMEM
S = pltpu.SMEM
H = pltpu.HBM


def iota(shape, dim):
    return lax.broadcasted_iota(i32, shape, dim)


def call(body, outs, ins, name, scratch=(), vmem=53, flops=10**6, nbytes=10**6):
    return pl.pallas_call(
        body,
        out_shape=[jax.ShapeDtypeStruct(shape, dtype) for shape, dtype, *_ in outs],
        in_specs=[pl.BlockSpec(memory_space=space) for space, _ in ins],
        out_specs=[pl.BlockSpec(memory_space=out[2] if len(out) > 2 else V) for out in outs],
        scratch_shapes=list(scratch),
        compiler_params=pltpu.CompilerParams(vmem_limit_bytes=vmem * MIB),
        cost_estimate=pl.CostEstimate(flops=flops, bytes_accessed=nbytes, transcendentals=0),
        name=name,
    )(*[x for _, x in ins])


def reverse_lanes(x):
    return jnp.take_along_axis(x, 127 - iota(x.shape, 1), axis=1)


def fold_sign(planes):
    kind = iota((planes, CW), 0) // K
    return jnp.where((kind == 2) | (kind == 3) | (kind >= F), -1.0, 1.0).astype(f32)


def where_am_i():
    at = lax.axis_index("lat")
    return at & 1 == 1, at == lax.axis_size("lat") - 1, at == 0


def partners():
    i, j = lax.axis_index("lon"), lax.axis_index("lat")
    n, m = lax.axis_size("lon"), lax.axis_size("lat")
    top = j == m - 1
    to_east, to_west = lax.rem(i + 1, n), lax.rem(i + n - 1, n)
    north_of, south_of = jnp.minimum(j + 1, m - 1), jnp.maximum(j - 1, 0)
    return (
        jnp.where(top, lax.rem(2 * n - 2 - i, n), to_east) * m + north_of,
        jnp.where(top, lax.rem(n - i, n), to_west) * m + north_of,
        to_east * m + south_of,
        to_west * m + south_of,
    )


def corner_rows(blocks, line, place):
    lane = iota((8, CW), 1)
    row = jnp.zeros((8, CW), f32)
    for f in range(F - 1):
        row = jnp.where(lane & 3 == f, pltpu.roll(blocks[f], (f - place) % CW, axis=1), row)
    picked = (4 * (lane - TAIL) + place) & (CW - 1)
    tail = jnp.take_along_axis(blocks[F - 1], picked, axis=1)
    return tail[line : line + 1], row[line : line + 1]


def post_corners(pay, rows, bottom):
    tail = iota((1, CW), 1) >= TAIL
    for n, at in enumerate(partners()):
        @pl.when(jnp.logical_not(bottom) if n >= 2 else at >= 0)
        def _(n=n, at=at):
            to = pl.ds(MESSAGE * at, 1)
            pay[to, :] = jnp.where(tail, rows[n][0], pay[to, :])
            pay[pl.ds(MESSAGE * at + 1, 1), :] = rows[n][1]


def corner_line(got, f, first, second):
    lane = iota((8, CW), 1)
    ats = partners()
    line = jnp.zeros((8, CW), f32)
    for place, n in ((1, first), (2, second)):
        row = got[pl.ds(MESSAGE * ats[n] + (0 if f == F - 1 else 1), 1), :]
        row = jnp.broadcast_to(row, (8, CW))
        if f == F - 1:
            moved = jnp.take_along_axis(row, TAIL + (lane >> 2), axis=1)
        else:
            moved = pltpu.roll(row, (place - f) % CW, axis=1)
        line = jnp.where(lane & 3 == place, moved, line)
    return line[:1]


NE, NW, SE, SW = range(4)
MESSAGE = 2
TAIL = CW - K
FLIPPED = (2, 3)


def thirds(x):
    pieces = []
    for _ in range(3):
        piece = x.astype(jnp.bfloat16)
        pieces.append(piece)
        x = x - piece.astype(f32)
    return pieces


def edges_kernel(x, vel, own, pay1, pay2, held, sems):
    odd, top, _ = where_am_i()
    copies = []
    for kind in range(F + 2):
        ref, plane = (x, kind * K) if kind < F else (vel, (kind - F) * K)
        copies.append(
            pltpu.make_async_copy(
                ref.at[pl.ds(plane * CL, K * CL)],
                held.at[pl.ds(kind * K * CL, K * CL)],
                sems.at[kind],
            )
        )
    for copy in copies:
        copy.start()
    group = iota((CL, CW), 1) >> 2
    for kind in range(F + 2):
        copies[kind].wait()
        for d in range(2 if kind < F else 1):
            low = held[pl.ds(kind * K * CL + d, K, stride=CL), :]
            high = held[pl.ds(kind * K * CL + CL - 1 - d, K, stride=CL), :]
            to = slice(d * ALL + kind * K, d * ALL + kind * K + K)
            pay1[to, :] = jnp.where(odd, low, high)
            pay2[to, :] = jnp.where(odd, high, low)

        def step(level, packed):
            rows = held[pl.ds(pl.multiple_of((kind * K + level) * CL, CL), CL), :]
            moved = pltpu.roll(rows, 4 * level + 2, axis=1)
            return jnp.where(group == level, moved, packed)

        own[kind] = lax.fori_loop(0, K, step, jnp.zeros((CL, CW), f32), unroll=True)

    @pl.when(top)
    def _():
        pay2[:ALL, :] = fold_sign(ALL) * reverse_lanes(pay2[:ALL, :])
        pay2[ALL:, :] = fold_sign(PLANES) * reverse_lanes(pay2[ALL:, :])


def halo_rows(got1, got2, odd):
    near, far = slice(0, ALL), slice(ALL, ALL + PLANES)
    norths = [jnp.where(odd, got2[cut, :], got1[cut, :]) for cut in (near, far)]
    souths = [jnp.where(odd, got1[cut, :], got2[cut, :]) for cut in (near, far)]
    return norths + souths


def spread(line):
    level, lane = iota((K, CW), 0), iota((K, CW), 1)
    return jnp.take_along_axis(
        jnp.broadcast_to(line, (K, CW)), (lane + 4 * level + 2) & (CW - 1), axis=1
    )


def gather_line(rows):
    level, lane = iota((K, CW), 0), iota((K, CW), 1)
    moved = jnp.take_along_axis(rows, (lane - 4 * level - 2) & (CW - 1), axis=1)
    return jnp.sum(jnp.where(lane >> 2 == level, moved, 0.0), axis=0, keepdims=True)


def north(x):
    return pltpu.roll(x, EXT - 1, axis=0)


def south(x):
    return pltpu.roll(x, 1, axis=0)


def east(x):
    return pltpu.roll(x, CW - 1, axis=1)


def west(x):
    return pltpu.roll(x, 1, axis=1)


def swapped(x, slot):
    return jnp.where(slot == 1, east(x), jnp.where(slot == 2, west(x), x))


def parts(u, v):
    return (
        1.0 - jnp.abs(u) - jnp.abs(v),
        -jnp.minimum(u, 0.0),
        jnp.maximum(u, 0.0),
        -jnp.minimum(v, 0.0),
        jnp.maximum(v, 0.0),
    )


def pack_kernel(counts, value, weight, owner, cell, own, pay, slots):
    dest = iota((NDEV, 128), 0)
    lane = iota((1, 128), 1)
    before = (iota((128, 128), 0) < iota((128, 128), 1)).astype(f32).astype(jnp.bfloat16)
    ones = jnp.ones((128, 128), jnp.bfloat16)
    carry = jnp.zeros((NDEV, 128), f32)
    total = jnp.zeros((NDEV, 128), f32)
    place = iota((CAP, 128), 0).astype(f32)
    for b in range(NBLK):
        live = lane < counts[0, b]
        who = jnp.where(live, owner[b : b + 1, :], -1)
        hot = (dest == who).astype(f32)
        hot16 = hot.astype(jnp.bfloat16)
        earlier = carry + jnp.dot(hot16, before, preferred_element_type=f32)
        carry = carry + jnp.dot(hot16, ones, preferred_element_type=f32)
        slot = jnp.sum(hot * earlier, axis=0, keepdims=True)
        slot = jnp.where(live, slot, -1.0)
        slots[b : b + 1, :] = slot
        code = (cell[b : b + 1, :] + (b % (STEPS + 1)) * (ROWS * CW)).astype(f32)
        here = place == slot
        fields = [
            jnp.where(here, data, 0.0) for data in (value[b : b + 1, :], weight[b : b + 1, :], code)
        ]
        fields.append(jnp.zeros((128 - 3 * CAP, 128), f32))
        total = total + lax.dot_general(
            jnp.concatenate([hot16] * 3, axis=1),
            jnp.concatenate(thirds(jnp.concatenate(fields, axis=0)), axis=1),
            (((1,), (1,)), ((), ())),
            preferred_element_type=f32,
        )
    pay[...] = jnp.zeros(pay.shape, f32)
    pay[pl.ds(0, NDEV, stride=MESSAGE), :] = total
    low = [own[f, :8, :] for f in range(F)]
    high = [own[f, CL - 8 :, :] for f in range(F)]
    _, _, bottom = where_am_i()
    post_corners(
        pay,
        [
            corner_rows(high, 7, 1),
            corner_rows(high, 7, 2),
            corner_rows(low, 0, 1),
            corner_rows(low, 0, 2),
        ],
        bottom,
    )


PAD = 8
GROUP = 8
UNROLL = 8
TILES = CL // 8


def core_kernel(kap, arrived, x, vel_in, got1, got2, own, from_west, from_east,
                replies, forecast, part, pay1, pay2, spill,
                states, forcing, vel, rows_of, adds, cell_of, index_v, index_s,
                halo, edge, side, mine_all, beside, beside1, own_f, own_a, sems):
    odd, top, bottom = where_am_i()
    load_x = pltpu.make_async_copy(x, states.at[pl.ds(PAD, ROWS)], sems.at[0])
    load_x.start()
    load_v = pltpu.make_async_copy(vel_in, vel.at[pl.ds(PAD, 2 * K * CL)], sems.at[1])
    load_v.start()
    box = arrived[pl.ds(0, NDEV, stride=MESSAGE), :]
    index_v[...] = (jnp.transpose(box)[2 * CAP : 3 * CAP].astype(i32) >> 7) + PAD
    load_i = pltpu.make_async_copy(index_v, index_s, sems.at[2])
    load_i.start()

    lane = iota((EXT, CW), 1)
    slot = lane & 3
    for n, rows in enumerate(halo_rows(got1, got2, odd)):
        halo[n, : rows.shape[0], :] = rows
    near_slot = iota((CL, CW), 1) & 3
    for kind in range(F + 2):
        side[kind, :CL, :] = jnp.where(near_slot < 2, from_west[kind], from_east[kind])
        side[kind, CL:, :] = jnp.zeros((8, CW), f32)
        mine_all[kind, :CL, :] = own[kind]
        mine_all[kind, CL:, :] = jnp.zeros((8, CW), f32)
        span = slice(kind * K, kind * K + K)
        mine_all[kind, CL : CL + 1, :] = gather_line(halo[0, span, :])
        mine_all[kind, EXT - 1 :, :] = gather_line(halo[2, span, :])
        if kind < F:
            line = corner_line(arrived, kind, NW, NE)
            side[kind, CL : CL + 1, :] = jnp.where(top, -line, line) if kind in FLIPPED else line
            line = corner_line(arrived, kind, SW, SE)
            side[kind, EXT - 1 :, :] = jnp.where(bottom, 0.0, line)
    base, um, up, vm, vp = parts(side[F], side[F + 1])
    for f in range(F):
        k = kap[f]
        mine = mine_all[f]
        near = side[f]
        e = jnp.where(slot == 1, east(mine), east(near))
        w = jnp.where(slot == 1, west(near), west(mine))
        beside[f] = swapped(near, slot)
        next_near = (
            (base - 4.0 * k) * near
            + (k + um) * e
            + (k + up) * w
            + (k + vm) * north(near)
            + (k + vp) * south(near)
        )
        beside1[f] = swapped(next_near, slot)

    @pl.loop(0, 3 * ROWS // 256)
    def _(i):
        forcing[pl.ds(pl.multiple_of(i * 256, 256) + PAD, 256), :] = jnp.zeros((256, CW), f32)

    first = iota((8, CW), 1) == 0
    last = iota((8, CW), 1) == CW - 1
    row0 = iota((8, CW), 0) == 0
    row7 = iota((8, CW), 0) == 7
    first_k = iota((K, CW), 1) == 0
    last_k = iota((K, CW), 1) == CW - 1
    NORTH, SOUTH = 0, 2
    load_x.wait()
    load_v.wait()

    def line(ref, row, f, base=0):
        return ref[pl.ds(PAD + base + f * K * CL + row, K, stride=CL), :]

    def span(f):
        return slice(f * K, f * K + K)

    for n, at, inner in ((NORTH, CL, CL - 1), (SOUTH, EXT - 1, 0)):
        base, um, up, vm, vp = parts(halo[n, span(F), :], halo[n, span(F + 1), :])
        for f in range(F):
            k = kap[f]
            a = halo[n, span(f), :]
            far = halo[n + 1, span(f), :]
            close = line(states, inner, f)
            to_north, to_south = (far, close) if n == NORTH else (close, far)
            h = spread(side[f, at : at + 1, :])
            b = (
                (base - 4.0 * k) * a
                + (k + um) * east(jnp.where(first_k, h, a))
                + (k + up) * west(jnp.where(last_k, h, a))
                + (k + vm) * to_north
                + (k + vp) * to_south
            )
            if n == SOUTH:
                b = jnp.where(bottom, 0.0, b)
            edge[n // 2, span(f), :] = b

    def around(ref, start, t, north_row, south_row):
        at = start + 8 * t
        a = ref[pl.ds(pl.multiple_of(at, 8), 8), :]
        n = ref[pl.ds(at + 1, 8), :]
        s = ref[pl.ds(at - 1, 8), :]
        if t == TILES - 1:
            n = jnp.where(row7, north_row, n)
        if t == 0:
            s = jnp.where(row0, south_row, s)
        return a, n, s

    def forward(source, target, packed, north_of, south_of):
        @pl.loop(0, K, unroll=UNROLL)
        def _(level):
            turn = 126 - 4 * level
            for t in range(TILES):
                at = pl.multiple_of(PAD + level * CL, 8) + 8 * t
                u = vel[pl.ds(pl.multiple_of(at, 8), 8), :]
                v = vel[pl.ds(pl.multiple_of(at + K * CL, 8), 8), :]
                base, um, up, vm, vp = parts(u, v)
                for f in range(F):
                    k = kap[f]
                    plane = f * K + level
                    start = PAD + source * ROWS + plane * CL
                    a, n, s = around(states, start, t, north_of(plane), south_of(plane))
                    h = pltpu.roll(packed[f, 8 * t : 8 * t + 8, :], turn, axis=1)
                    b = (
                        (base - 4.0 * k) * a
                        + (k + um) * jnp.where(last, h, east(a))
                        + (k + up) * jnp.where(first, h, west(a))
                        + (k + vm) * n
                        + (k + vp) * s
                    )
                    to = PAD + target * ROWS + plane * CL + 8 * t
                    states[pl.ds(pl.multiple_of(to, 8), 8), :] = b

    def halo_row(n):
        return lambda plane: halo[n, pl.ds(plane, 1), :]

    def edge_row(n):
        return lambda plane: edge[n, pl.ds(plane, 1), :]

    forward(0, 1, beside, halo_row(NORTH), halo_row(SOUTH))
    forward(1, 2, beside1, edge_row(0), edge_row(1))
    save = pltpu.make_async_copy(states.at[pl.ds(PAD + 2 * ROWS, ROWS)], forecast, sems.at[3])
    save.start()

    load_i.wait()

    @pl.loop(0, NDEV, unroll=4)
    def _(s):
        for q in range(CAP):
            at = index_s[q, s]
            rows_of[pl.ds(q * NDEV + s, 1), :] = states[pl.ds(at, 1), :]

    lane_s = iota((NDEV, CW), 1)
    cells = box.astype(i32)
    ones = jnp.ones((3 * CW, CW), jnp.bfloat16)
    modelled = jnp.zeros((NDEV, CW), f32)
    for q in range(CAP):
        cut = slice(q * NDEV, (q + 1) * NDEV)
        cell = jnp.broadcast_to(cells[:, 2 * CAP + q : 2 * CAP + q + 1], (NDEV, CW))
        cell_of[cut, :] = cell
        seen = jnp.where(lane_s == cell & (CW - 1), rows_of[cut, :], 0.0)
        seen = jnp.dot(
            jnp.concatenate(thirds(seen), axis=1), ones, preferred_element_type=f32
        )
        modelled = jnp.where(lane_s == q, seen, modelled)
    weight = pltpu.roll(box, CW - CAP, axis=1)
    result = jnp.where(lane_s < CAP, weight * (box - modelled), 0.0)
    replies[...] = jnp.zeros(replies.shape, f32)
    replies[pl.ds(0, NDEV, stride=MESSAGE), :] = result
    for start in range(0, CAP, GROUP):
        for q in range(start, start + GROUP):
            cut = slice(q * NDEV, (q + 1) * NDEV)
            dep = jnp.broadcast_to(result[:, q : q + 1], (NDEV, CW))
            adds[cut, :] = jnp.where(lane_s == cell_of[cut, :] & (CW - 1), dep, 0.0)
        for q in range(start + GROUP - 1, start, -1):
            cut = slice(q * NDEV, (q + 1) * NDEV)
            mine = cell_of[cut, :] >> 7
            acc = adds[cut, :]
            for p in range(start, q):
                other = slice(p * NDEV, (p + 1) * NDEV)
                acc = acc + jnp.where(mine == cell_of[other, :] >> 7, adds[other, :], 0.0)
            adds[cut, :] = acc

    @pl.loop(0, NDEV, unroll=4)
    def _(s):
        for start in range(0, CAP, GROUP):
            ats = [index_s[q, s] for q in range(start, start + GROUP)]
            olds = [forcing[pl.ds(at, 1), :] for at in ats]
            for n in range(GROUP):
                forcing[pl.ds(ats[n], 1), :] = (
                    olds[n] + adds[pl.ds((start + n) * NDEV + s, 1), :]
                )

    own_f[...] = jnp.zeros(own_f.shape, f32)
    own_a[...] = jnp.zeros(own_a.shape, f32)
    group = iota((8, CW), 1) >> 2

    @pl.loop(0, K, unroll=UNROLL)
    def _(level):
        here = group == level
        turn = 4 * level + 2
        for t in range(TILES):
            at = pl.multiple_of(PAD + level * CL, 8) + 8 * t
            u = vel[pl.ds(pl.multiple_of(at, 8), 8), :]
            v, vn, vs = around(vel, PAD + (K + level) * CL, t, 0.0, 0.0)
            base, um, up, _, _ = parts(u, v)
            vm = -jnp.minimum(vs, 0.0)
            vp = jnp.maximum(vn, 0.0)
            cut = slice(8 * t, 8 * t + 8)
            for f in range(F):
                k = kap[f]
                plane = f * K + level
                a, n, s = around(forcing, PAD + 2 * ROWS + plane * CL, t, 0.0, 0.0)
                own_f[f, cut, :] = jnp.where(here, pltpu.roll(a, turn, axis=1), own_f[f, cut, :])
                to = pl.ds(pl.multiple_of(PAD + ROWS + plane * CL + 8 * t, 8), 8)
                more = forcing[to, :]
                own_a[f, cut, :] = jnp.where(here, pltpu.roll(more, turn, axis=1), own_a[f, cut, :])
                b = (
                    (base - 4.0 * k) * a
                    + jnp.where(first, 0.0, west((k + um) * a))
                    + jnp.where(last, 0.0, east((k + up) * a))
                    + (k + vm) * s
                    + (k + vp) * n
                    + more
                )
                forcing[to, :] = b

    for n, at, inner in ((NORTH, CL, CL - 1), (SOUTH, EXT - 1, 0)):
        hu, hv = halo[n, span(F), :], halo[n, span(F + 1), :]
        base, um, up, vm, vp = parts(hu, hv)
        nearest = line(vel, inner, 1)
        push = jnp.maximum(nearest, 0.0) if n == SOUTH else -jnp.minimum(nearest, 0.0)
        on = vp if n == SOUTH else vm
        for f in range(F):
            k = kap[f]
            b = (k + push) * line(forcing, inner, f, 2 * ROWS)
            if n == SOUTH:
                b = jnp.where(bottom, 0.0, b)
            edge[n // 2, span(f), :] = b
            near = (
                (base - 4.0 * k) * b
                + jnp.where(first_k, 0.0, west((k + um) * b))
                + jnp.where(last_k, 0.0, east((k + up) * b))
                + (k + push) * line(forcing, inner, f, ROWS)
            )
            for d, rows in ((0, near), (1, (k + on) * b)):
                to = slice(d * PLANES + f * K, d * PLANES + f * K + K)
                mirrored = reverse_lanes(rows)
                mirrored = -mirrored if f in FLIPPED else mirrored
                if n == NORTH:
                    pay1[to, :] = rows
                    pay2[to, :] = jnp.where(top, mirrored, rows)
                else:
                    pay1[to, :] = jnp.where(odd, rows, pay1[to, :])
                    pay2[to, :] = jnp.where(odd, pay2[to, :], rows)

    base, um, up, vm, vp = parts(side[F], side[F + 1])
    obase, oum, oup, ovm, ovp = parts(mine_all[F], mine_all[F + 1])
    gone = bottom & (iota((EXT, CW), 0) >= CL + 2)
    ends = []
    for f in range(F):
        k = kap[f]
        a = own_f[f]
        oa, ob = (k + oum) * a, (k + oup) * a
        b = jnp.where(slot == 1, east(ob), jnp.where(slot == 2, west(oa), 0.0))
        a = (
            (obase - 4.0 * k) * a
            + jnp.where(slot == 1, west(oa), east(ob))
            + south((k + ovm) * a)
            + north((k + ovp) * a)
        )
        a = jnp.where(gone, 0.0, a) + own_a[f]
        pa = (k + um) * b
        pb = (k + up) * b
        beside1[f] = swapped(jnp.where(slot == 1, pa, pb), slot)
        inner = (
            (base - 4.0 * k) * b
            + south((k + vm) * b)
            + north((k + vp) * b)
            + jnp.where(slot == 1, east((k + oup) * a), west((k + oum) * a))
        )
        outer = jnp.where(slot == 0, east(pb), west(pa))
        beyond = jnp.where((slot == 1) | (slot == 2), inner, outer)
        spill[f] = beyond[:CL]
        ends.append(beyond[CL:])
    post_corners(
        replies,
        [
            corner_rows(ends, 0, 2),
            corner_rows(ends, 0, 1),
            corner_rows(ends, 7, 2),
            corner_rows(ends, 7, 1),
        ],
        bottom,
    )

    def step(level):
        turn = 126 - 4 * level
        for t in range(TILES):
            at = pl.multiple_of(PAD + level * CL, 8) + 8 * t
            u = vel[pl.ds(pl.multiple_of(at, 8), 8), :]
            v, vn, vs = around(
                vel,
                PAD + (K + level) * CL,
                t,
                halo[NORTH, pl.ds((F + 1) * K + level, 1), :],
                halo[SOUTH, pl.ds((F + 1) * K + level, 1), :],
            )
            base, um, up, _, _ = parts(u, v)
            vm = -jnp.minimum(vs, 0.0)
            vp = jnp.maximum(vn, 0.0)
            for f in range(F):
                k = kap[f]
                plane = f * K + level
                start = PAD + ROWS + plane * CL
                a, n, s = around(forcing, start, t, edge_row(0)(plane), edge_row(1)(plane))
                h = pltpu.roll(beside1[f, 8 * t : 8 * t + 8, :], turn, axis=1)
                b = (
                    (base - 4.0 * k) * a
                    + jnp.where(first, h, west((k + um) * a))
                    + jnp.where(last, h, east((k + up) * a))
                    + (k + vm) * s
                    + (k + vp) * n
                    + forcing[pl.ds(pl.multiple_of(PAD + plane * CL + 8 * t, 8), 8), :]
                )
                forcing[pl.ds(pl.multiple_of(PAD + plane * CL + 8 * t, 8), 8), :] = b

    saves = [save]
    for half in range(2):
        pl.loop(half * (K // 2), (half + 1) * (K // 2), unroll=UNROLL)(step)
        for f in range(F):
            at = f * K * CL + half * (K // 2) * CL
            size = K // 2 * CL
            saves.append(
                pltpu.make_async_copy(
                    forcing.at[pl.ds(PAD + at, size)],
                    part.at[pl.ds(at, size)],
                    sems.at[4 + half * F + f],
                )
            )
            saves[-1].start()
    for copy in saves:
        copy.wait()


def finish_kernel(part, from_west, from_east, got1, got2, returned, owner, slots,
                  adjoint, departures, held, sems):
    size = K * CL
    loads, saves = [], []
    for f in range(F):
        cut = pl.ds(f * size, size)
        loads.append(pltpu.make_async_copy(part.at[cut], held.at[cut], sems.at[f]))
        saves.append(pltpu.make_async_copy(held.at[cut], adjoint.at[cut], sems.at[F + f]))
        loads[f].start()

    flat = jnp.transpose(returned[pl.ds(0, NDEV, stride=MESSAGE), :])[:CAP]
    flat = jnp.concatenate(thirds(flat), axis=0)
    dest = iota((NDEV, 128), 0)
    place = iota((CAP, 128), 0).astype(f32)
    for b in range(NBLK):
        hot = (dest == owner[b : b + 1, :]).astype(f32).astype(jnp.bfloat16)
        found = jnp.dot(flat, hot, preferred_element_type=f32)
        found = found[:CAP] + found[CAP : 2 * CAP] + found[2 * CAP :]
        departures[b : b + 1, :] = jnp.sum(
            jnp.where(place == slots[b : b + 1, :], found, 0.0), axis=0, keepdims=True
        )

    odd, top, bottom = where_am_i()
    lane = iota((CL, CW), 1)
    slot = lane & 3
    close = (lane < 2) | (lane >= CW - 2)
    for f in range(F):
        merged = jnp.where(slot < 2, from_east[f], from_west[f])
        loads[f].wait()

        @pl.loop(0, K, unroll=K)
        def _(level):
            more = pltpu.roll(merged, 126 - 4 * level, axis=1)
            at = pl.multiple_of((f * K + level) * CL, CL)
            held[pl.ds(at, CL), :] = held[pl.ds(at, CL), :] + jnp.where(close, more, 0.0)

        north_line = corner_line(returned, f, NE, NW)
        north_line = jnp.where(top, -north_line, north_line) if f in FLIPPED else north_line
        south_line = jnp.where(bottom, 0.0, corner_line(returned, f, SE, SW))
        for d in range(2):
            cut = slice(d * PLANES + f * K, d * PLANES + f * K + K)
            more_up = jnp.where(odd, got2[cut, :], got1[cut, :])
            more_down = jnp.where(odd, got1[cut, :], got2[cut, :])
            if d == 0:
                more_up = more_up + jnp.where(close, spread(north_line), 0.0)
                more_down = more_down + jnp.where(close, spread(south_line), 0.0)
            up = pl.ds(f * size + CL - 1 - d, K, stride=CL)
            held[up, :] = held[up, :] + more_up
            down = pl.ds(f * size + d, K, stride=CL)
            held[down, :] = held[down, :] + more_down
        saves[f].start()
    for copy in saves:
        copy.wait()


def all_to_all(x):
    shape = x.shape
    x = x.reshape(NDEV, 1, MESSAGE * CW)
    x = lax.all_to_all(x, ("lon", "lat"), split_axis=0, concat_axis=0, tiled=True)
    return x.reshape(shape)


def shards(
    background, velocity, diffusivity, obs_value, obs_weight, obs_owner, obs_counts, obs_cell
):
    nlon = lax.axis_size("lon")
    nlat = lax.axis_size("lat")
    both = ("lon", "lat")

    def number(i, j):
        return i * nlat + j

    pairs1 = [(number(i, j), number(i, j ^ 1)) for i in range(nlon) for j in range(nlat)]
    pairs2 = []
    for i in range(nlon):
        for j in range(1, nlat - 1):
            pairs2.append((number(i, j), number(i, j + 1 if j & 1 else j - 1)))
        pairs2.append((number(i, nlat - 1), number(nlon - 1 - i, nlat - 1)))
    eastward = [(i, (i + 1) % nlon) for i in range(nlon)]
    westward = [((i + 1) % nlon, i) for i in range(nlon)]

    def around(x):
        return lax.ppermute(x, "lon", eastward), lax.ppermute(x, "lon", westward)

    x = background.reshape(ROWS, CW)
    vel = velocity.reshape(2 * K * CL, CW)
    own, pay1, pay2 = call(
        edges_kernel,
        [((F + 2, CL, CW), f32)] + [((ALL + PLANES, CW), f32)] * 2,
        [(H, x), (H, vel)],
        "edges",
        scratch=[V((ALL * CL, CW), f32), pltpu.SemaphoreType.DMA((F + 2,))],
    )
    got2 = lax.ppermute(pay2, both, pairs2)
    from_west, from_east = around(own)

    owner = obs_owner.reshape(NBLK, 128)
    packed, slots = call(
        pack_kernel,
        [((MESSAGE * NDEV, CW), f32), ((NBLK, 128), f32)],
        [
            (S, obs_counts),
            (V, obs_value.reshape(NBLK, 128)),
            (V, obs_weight.reshape(NBLK, 128)),
            (V, owner),
            (V, obs_cell.reshape(NBLK, 128)),
            (V, own),
        ],
        "pack",
    )
    pay1, packed = lax.optimization_barrier((pay1, packed))
    got1 = lax.ppermute(pay1, both, pairs1)
    arrived = all_to_all(packed)
    padded = 3 * ROWS + 2 * PAD
    replies, forecast, part, pay1, pay2, spill = call(
        core_kernel,
        [
            ((MESSAGE * NDEV, CW), f32),
            ((ROWS, CW), f32, H),
            ((ROWS, CW), f32, H),
            ((2 * PLANES, CW), f32),
            ((2 * PLANES, CW), f32),
            ((F, CL, CW), f32),
        ],
        [
            (S, diffusivity),
            (V, arrived),
            (H, x),
            (H, vel),
            (V, got1),
            (V, got2),
            (V, own),
            (V, from_west),
            (V, from_east),
        ],
        "core",
        vmem=52,
        scratch=[
            V((padded, CW), f32),
            V((padded, CW), f32),
            V((2 * K * CL + 2 * PAD, CW), f32),
            V((CAP * NDEV, CW), f32),
            V((CAP * NDEV, CW), f32),
            V((CAP * NDEV, CW), i32),
            V((CAP, 128), i32),
            S((CAP, 128), i32),
            V((4, ALL, CW), f32),
            V((2, PLANES, CW), f32),
            V((F + 2, EXT, CW), f32),
            V((F + 2, EXT, CW), f32),
            V((F, EXT, CW), f32),
            V((F, EXT, CW), f32),
            V((F, EXT, CW), f32),
            V((F, EXT, CW), f32),
            pltpu.SemaphoreType.DMA((4 + 2 * F,)),
        ],
    )
    back2 = lax.ppermute(pay2, both, pairs2)
    back1 = lax.ppermute(pay1, both, pairs1)
    spill_west, spill_east = around(spill)
    returned = all_to_all(replies)
    adjoint, found = call(
        finish_kernel,
        [((ROWS, CW), f32, H), ((NBLK, 128), f32)],
        [
            (H, part),
            (V, spill_west),
            (V, spill_east),
            (V, back1),
            (V, back2),
            (V, returned),
            (V, owner),
            (V, slots),
        ],
        "finish",
        scratch=[V((ROWS, CW), f32), pltpu.SemaphoreType.DMA((2 * F,))],
    )
    shape = (F, K, CL, CW)
    return forecast.reshape(shape), adjoint.reshape(shape), found.reshape(-1)


def solution(mesh):
    in_specs = (
        P(None, None, "lat", "lon"),
        P(None, None, "lat", "lon"),
        P(),
        P(("lon", "lat")),
        P(("lon", "lat")),
        P(("lon", "lat"), None),
        P(("lon", "lat"), None),
        P(("lon", "lat")),
    )
    out_specs = (P(None, None, "lat", "lon"), P(None, None, "lat", "lon"), P(("lon", "lat")))
    return jax.shard_map(shards, mesh=mesh, in_specs=in_specs, out_specs=out_specs, check_vma=False)
```

```python
import jax
import jax.numpy as jnp
from jax import lax
from jax.experimental import pallas as pl
from jax.experimental.pallas import tpu as pltpu
from jax.sharding import PartitionSpec as P


STEPS = 2
F = 5
K = 32
CL = 32
CW = 128
PLANES = F * K
ALL = PLANES + 2 * K
EXT = 40
ROWS = PLANES * CL
NBLK = 8
NDEV = 128
CAP = 16
MIB = 1 << 20
f32 = jnp.float32
i32 = jnp.int32


V = pltpu.VMEM
S = pltpu.SMEM
H = pltpu.HBM


def iota(shape, dim):
    return lax.broadcasted_iota(i32, shape, dim)


def call(body, outs, ins, name, scratch=(), vmem=53, flops=10**6, nbytes=10**6):
    return pl.pallas_call(
        body,
        out_shape=[jax.ShapeDtypeStruct(shape, dtype) for shape, dtype, *_ in outs],
        in_specs=[pl.BlockSpec(memory_space=space) for space, _ in ins],
        out_specs=[pl.BlockSpec(memory_space=out[2] if len(out) > 2 else V) for out in outs],
        scratch_shapes=list(scratch),
        compiler_params=pltpu.CompilerParams(vmem_limit_bytes=vmem * MIB),
        cost_estimate=pl.CostEstimate(flops=flops, bytes_accessed=nbytes, transcendentals=0),
        name=name,
    )(*[x for _, x in ins])


def reverse_lanes(x):
    return jnp.take_along_axis(x, 127 - iota(x.shape, 1), axis=1)


def fold_sign(planes):
    kind = iota((planes, CW), 0) // K
    return jnp.where((kind == 2) | (kind == 3) | (kind >= F), -1.0, 1.0).astype(f32)


def where_am_i():
    at = lax.axis_index("lat")
    return at & 1 == 1, at == lax.axis_size("lat") - 1, at == 0


def partners():
    i, j = lax.axis_index("lon"), lax.axis_index("lat")
    n, m = lax.axis_size("lon"), lax.axis_size("lat")
    top = j == m - 1
    to_east, to_west = lax.rem(i + 1, n), lax.rem(i + n - 1, n)
    north_of, south_of = jnp.minimum(j + 1, m - 1), jnp.maximum(j - 1, 0)
    return (
        jnp.where(top, lax.rem(2 * n - 2 - i, n), to_east) * m + north_of,
        jnp.where(top, lax.rem(n - i, n), to_west) * m + north_of,
        to_east * m + south_of,
        to_west * m + south_of,
    )


def corner_rows(blocks, line, place):
    lane = iota((8, CW), 1)
    row = jnp.zeros((8, CW), f32)
    for f in range(F - 1):
        row = jnp.where(lane & 3 == f, pltpu.roll(blocks[f], (f - place) % CW, axis=1), row)
    picked = (4 * (lane - TAIL) + place) & (CW - 1)
    tail = jnp.take_along_axis(blocks[F - 1], picked, axis=1)
    return tail[line : line + 1], row[line : line + 1]


def post_corners(pay, rows, bottom):
    tail = iota((1, CW), 1) >= TAIL
    for n, at in enumerate(partners()):
        @pl.when(jnp.logical_not(bottom) if n >= 2 else at >= 0)
        def _(n=n, at=at):
            to = pl.ds(MESSAGE * at, 1)
            pay[to, :] = jnp.where(tail, rows[n][0], pay[to, :])
            pay[pl.ds(MESSAGE * at + 1, 1), :] = rows[n][1]


def corner_line(got, f, first, second):
    lane = iota((8, CW), 1)
    ats = partners()
    line = jnp.zeros((8, CW), f32)
    for place, n in ((1, first), (2, second)):
        row = got[pl.ds(MESSAGE * ats[n] + (0 if f == F - 1 else 1), 1), :]
        row = jnp.broadcast_to(row, (8, CW))
        if f == F - 1:
            moved = jnp.take_along_axis(row, TAIL + (lane >> 2), axis=1)
        else:
            moved = pltpu.roll(row, (place - f) % CW, axis=1)
        line = jnp.where(lane & 3 == place, moved, line)
    return line[:1]


NE, NW, SE, SW = range(4)
MESSAGE = 2
TAIL = CW - K
FLIPPED = (2, 3)


def thirds(x):
    pieces = []
    for _ in range(3):
        piece = x.astype(jnp.bfloat16)
        pieces.append(piece)
        x = x - piece.astype(f32)
    return pieces


def edges_kernel(x, vel, own, pay1, pay2, held, sems):
    odd, top, _ = where_am_i()
    copies = []
    for kind in range(F + 2):
        ref, plane = (x, kind * K) if kind < F else (vel, (kind - F) * K)
        copies.append(
            pltpu.make_async_copy(
                ref.at[pl.ds(plane * CL, K * CL)],
                held.at[pl.ds(kind * K * CL, K * CL)],
                sems.at[kind],
            )
        )
    for copy in copies:
        copy.start()
    group = iota((CL, CW), 1) >> 2
    for kind in range(F + 2):
        copies[kind].wait()
        for d in range(2 if kind < F else 1):
            low = held[pl.ds(kind * K * CL + d, K, stride=CL), :]
            high = held[pl.ds(kind * K * CL + CL - 1 - d, K, stride=CL), :]
            to = slice(d * ALL + kind * K, d * ALL + kind * K + K)
            pay1[to, :] = jnp.where(odd, low, high)
            pay2[to, :] = jnp.where(odd, high, low)

        def step(level, packed):
            rows = held[pl.ds(pl.multiple_of((kind * K + level) * CL, CL), CL), :]
            moved = pltpu.roll(rows, 4 * level + 2, axis=1)
            return jnp.where(group == level, moved, packed)

        own[kind] = lax.fori_loop(0, K, step, jnp.zeros((CL, CW), f32), unroll=True)

    @pl.when(top)
    def _():
        pay2[:ALL, :] = fold_sign(ALL) * reverse_lanes(pay2[:ALL, :])
        pay2[ALL:, :] = fold_sign(PLANES) * reverse_lanes(pay2[ALL:, :])


def halo_rows(got1, got2, odd):
    near, far = slice(0, ALL), slice(ALL, ALL + PLANES)
    norths = [jnp.where(odd, got2[cut, :], got1[cut, :]) for cut in (near, far)]
    souths = [jnp.where(odd, got1[cut, :], got2[cut, :]) for cut in (near, far)]
    return norths + souths


def spread(line):
    level, lane = iota((K, CW), 0), iota((K, CW), 1)
    return jnp.take_along_axis(
        jnp.broadcast_to(line, (K, CW)), (lane + 4 * level + 2) & (CW - 1), axis=1
    )


def gather_line(rows):
    level, lane = iota((K, CW), 0), iota((K, CW), 1)
    moved = jnp.take_along_axis(rows, (lane - 4 * level - 2) & (CW - 1), axis=1)
    return jnp.sum(jnp.where(lane >> 2 == level, moved, 0.0), axis=0, keepdims=True)


def north(x):
    return pltpu.roll(x, EXT - 1, axis=0)


def south(x):
    return pltpu.roll(x, 1, axis=0)


def east(x):
    return pltpu.roll(x, CW - 1, axis=1)


def west(x):
    return pltpu.roll(x, 1, axis=1)


def swapped(x, slot):
    return jnp.where(slot == 1, east(x), jnp.where(slot == 2, west(x), x))


def parts(u, v):
    return (
        1.0 - jnp.abs(u) - jnp.abs(v),
        -jnp.minimum(u, 0.0),
        jnp.maximum(u, 0.0),
        -jnp.minimum(v, 0.0),
        jnp.maximum(v, 0.0),
    )


def pack_kernel(counts, value, weight, owner, cell, own, pay, slots):
    dest = iota((NDEV, 128), 0)
    lane = iota((1, 128), 1)
    before = (iota((128, 128), 0) < iota((128, 128), 1)).astype(f32).astype(jnp.bfloat16)
    ones = jnp.ones((128, 128), jnp.bfloat16)
    carry = jnp.zeros((NDEV, 128), f32)
    total = jnp.zeros((NDEV, 128), f32)
    place = iota((CAP, 128), 0).astype(f32)
    for b in range(NBLK):
        live = lane < counts[0, b]
        who = jnp.where(live, owner[b : b + 1, :], -1)
        hot = (dest == who).astype(f32)
        hot16 = hot.astype(jnp.bfloat16)
        earlier = carry + jnp.dot(hot16, before, preferred_element_type=f32)
        carry = carry + jnp.dot(hot16, ones, preferred_element_type=f32)
        slot = jnp.sum(hot * earlier, axis=0, keepdims=True)
        slot = jnp.where(live, slot, -1.0)
        slots[b : b + 1, :] = slot
        code = (cell[b : b + 1, :] + (b % (STEPS + 1)) * (ROWS * CW)).astype(f32)
        here = place == slot
        fields = [
            jnp.where(here, data, 0.0) for data in (value[b : b + 1, :], weight[b : b + 1, :], code)
        ]
        fields.append(jnp.zeros((128 - 3 * CAP, 128), f32))
        total = total + lax.dot_general(
            jnp.concatenate([hot16] * 3, axis=1),
            jnp.concatenate(thirds(jnp.concatenate(fields, axis=0)), axis=1),
            (((1,), (1,)), ((), ())),
            preferred_element_type=f32,
        )
    pay[...] = jnp.zeros(pay.shape, f32)
    pay[pl.ds(0, NDEV, stride=MESSAGE), :] = total
    low = [own[f, :8, :] for f in range(F)]
    high = [own[f, CL - 8 :, :] for f in range(F)]
    _, _, bottom = where_am_i()
    post_corners(
        pay,
        [
            corner_rows(high, 7, 1),
            corner_rows(high, 7, 2),
            corner_rows(low, 0, 1),
            corner_rows(low, 0, 2),
        ],
        bottom,
    )


PAD = 8
GROUP = 8
UNROLL = 16
TILES = CL // 8


def core_kernel(kap, arrived, x, vel_in, got1, got2, own, from_west, from_east,
                replies, forecast, part, pay1, pay2, spill,
                states, forcing, vel, rows_of, adds, cell_of, index_v, index_s,
                halo, edge, side, mine_all, beside, beside1, own_f, own_a, sems):
    odd, top, bottom = where_am_i()
    load_x = pltpu.make_async_copy(x, states.at[pl.ds(PAD, ROWS)], sems.at[0])
    load_x.start()
    load_v = pltpu.make_async_copy(vel_in, vel.at[pl.ds(PAD, 2 * K * CL)], sems.at[1])
    load_v.start()
    box = arrived[pl.ds(0, NDEV, stride=MESSAGE), :]
    index_v[...] = (jnp.transpose(box)[2 * CAP : 3 * CAP].astype(i32) >> 7) + PAD
    load_i = pltpu.make_async_copy(index_v, index_s, sems.at[2])
    load_i.start()

    lane = iota((EXT, CW), 1)
    slot = lane & 3
    for n, rows in enumerate(halo_rows(got1, got2, odd)):
        halo[n, : rows.shape[0], :] = rows
    near_slot = iota((CL, CW), 1) & 3
    for kind in range(F + 2):
        side[kind, :CL, :] = jnp.where(near_slot < 2, from_west[kind], from_east[kind])
        side[kind, CL:, :] = jnp.zeros((8, CW), f32)
        mine_all[kind, :CL, :] = own[kind]
        mine_all[kind, CL:, :] = jnp.zeros((8, CW), f32)
        span = slice(kind * K, kind * K + K)
        mine_all[kind, CL : CL + 1, :] = gather_line(halo[0, span, :])
        mine_all[kind, EXT - 1 :, :] = gather_line(halo[2, span, :])
        if kind < F:
            line = corner_line(arrived, kind, NW, NE)
            side[kind, CL : CL + 1, :] = jnp.where(top, -line, line) if kind in FLIPPED else line
            line = corner_line(arrived, kind, SW, SE)
            side[kind, EXT - 1 :, :] = jnp.where(bottom, 0.0, line)
    base, um, up, vm, vp = parts(side[F], side[F + 1])
    for f in range(F):
        k = kap[f]
        mine = mine_all[f]
        near = side[f]
        e = jnp.where(slot == 1, east(mine), east(near))
        w = jnp.where(slot == 1, west(near), west(mine))
        beside[f] = swapped(near, slot)
        next_near = (
            (base - 4.0 * k) * near
            + (k + um) * e
            + (k + up) * w
            + (k + vm) * north(near)
            + (k + vp) * south(near)
        )
        beside1[f] = swapped(next_near, slot)

    @pl.loop(0, 3 * ROWS // 256)
    def _(i):
        forcing[pl.ds(pl.multiple_of(i * 256, 256) + PAD, 256), :] = jnp.zeros((256, CW), f32)

    first = iota((8, CW), 1) == 0
    last = iota((8, CW), 1) == CW - 1
    row0 = iota((8, CW), 0) == 0
    row7 = iota((8, CW), 0) == 7
    first_k = iota((K, CW), 1) == 0
    last_k = iota((K, CW), 1) == CW - 1
    NORTH, SOUTH = 0, 2
    load_x.wait()
    load_v.wait()

    def line(ref, row, f, base=0):
        return ref[pl.ds(PAD + base + f * K * CL + row, K, stride=CL), :]

    def span(f):
        return slice(f * K, f * K + K)

    for n, at, inner in ((NORTH, CL, CL - 1), (SOUTH, EXT - 1, 0)):
        base, um, up, vm, vp = parts(halo[n, span(F), :], halo[n, span(F + 1), :])
        for f in range(F):
            k = kap[f]
            a = halo[n, span(f), :]
            far = halo[n + 1, span(f), :]
            close = line(states, inner, f)
            to_north, to_south = (far, close) if n == NORTH else (close, far)
            h = spread(side[f, at : at + 1, :])
            b = (
                (base - 4.0 * k) * a
                + (k + um) * east(jnp.where(first_k, h, a))
                + (k + up) * west(jnp.where(last_k, h, a))
                + (k + vm) * to_north
                + (k + vp) * to_south
            )
            if n == SOUTH:
                b = jnp.where(bottom, 0.0, b)
            edge[n // 2, span(f), :] = b

    def around(ref, start, t, north_row, south_row):
        at = start + 8 * t
        a = ref[pl.ds(pl.multiple_of(at, 8), 8), :]
        n = ref[pl.ds(at + 1, 8), :]
        s = ref[pl.ds(at - 1, 8), :]
        if t == TILES - 1:
            n = jnp.where(row7, north_row, n)
        if t == 0:
            s = jnp.where(row0, south_row, s)
        return a, n, s

    def forward(source, target, packed, north_of, south_of):
        @pl.loop(0, K, unroll=UNROLL)
        def _(level):
            turn = 126 - 4 * level
            for t in range(TILES):
                at = pl.multiple_of(PAD + level * CL, 8) + 8 * t
                u = vel[pl.ds(pl.multiple_of(at, 8), 8), :]
                v = vel[pl.ds(pl.multiple_of(at + K * CL, 8), 8), :]
                base, um, up, vm, vp = parts(u, v)
                for f in range(F):
                    k = kap[f]
                    plane = f * K + level
                    start = PAD + source * ROWS + plane * CL
                    a, n, s = around(states, start, t, north_of(plane), south_of(plane))
                    h = pltpu.roll(packed[f, 8 * t : 8 * t + 8, :], turn, axis=1)
                    b = (
                        (base - 4.0 * k) * a
                        + (k + um) * jnp.where(last, h, east(a))
                        + (k + up) * jnp.where(first, h, west(a))
                        + (k + vm) * n
                        + (k + vp) * s
                    )
                    to = PAD + target * ROWS + plane * CL + 8 * t
                    states[pl.ds(pl.multiple_of(to, 8), 8), :] = b

    def halo_row(n):
        return lambda plane: halo[n, pl.ds(plane, 1), :]

    def edge_row(n):
        return lambda plane: edge[n, pl.ds(plane, 1), :]

    forward(0, 1, beside, halo_row(NORTH), halo_row(SOUTH))
    forward(1, 2, beside1, edge_row(0), edge_row(1))
    save = pltpu.make_async_copy(states.at[pl.ds(PAD + 2 * ROWS, ROWS)], forecast, sems.at[3])
    save.start()

    load_i.wait()

    @pl.loop(0, NDEV, unroll=8)
    def _(s):
        for q in range(CAP):
            at = index_s[q, s]
            rows_of[pl.ds(q * NDEV + s, 1), :] = states[pl.ds(at, 1), :]

    lane_s = iota((NDEV, CW), 1)
    cells = box.astype(i32)
    ones = jnp.ones((3 * CW, CW), jnp.bfloat16)
    modelled = jnp.zeros((NDEV, CW), f32)
    for q in range(CAP):
        cut = slice(q * NDEV, (q + 1) * NDEV)
        cell = jnp.broadcast_to(cells[:, 2 * CAP + q : 2 * CAP + q + 1], (NDEV, CW))
        cell_of[cut, :] = cell
        seen = jnp.where(lane_s == cell & (CW - 1), rows_of[cut, :], 0.0)
        seen = jnp.dot(
            jnp.concatenate(thirds(seen), axis=1), ones, preferred_element_type=f32
        )
        modelled = jnp.where(lane_s == q, seen, modelled)
    weight = pltpu.roll(box, CW - CAP, axis=1)
    result = jnp.where(lane_s < CAP, weight * (box - modelled), 0.0)
    replies[...] = jnp.zeros(replies.shape, f32)
    replies[pl.ds(0, NDEV, stride=MESSAGE), :] = result
    for start in range(0, CAP, GROUP):
        for q in range(start, start + GROUP):
            cut = slice(q * NDEV, (q + 1) * NDEV)
            dep = jnp.broadcast_to(result[:, q : q + 1], (NDEV, CW))
            adds[cut, :] = jnp.where(lane_s == cell_of[cut, :] & (CW - 1), dep, 0.0)
        for q in range(start + GROUP - 1, start, -1):
            cut = slice(q * NDEV, (q + 1) * NDEV)
            mine = cell_of[cut, :] >> 7
            acc = adds[cut, :]
            for p in range(start, q):
                other = slice(p * NDEV, (p + 1) * NDEV)
                acc = acc + jnp.where(mine == cell_of[other, :] >> 7, adds[other, :], 0.0)
            adds[cut, :] = acc

    @pl.loop(0, NDEV, unroll=8)
    def _(s):
        for start in range(0, CAP, GROUP):
            ats = [index_s[q, s] for q in range(start, start + GROUP)]
            olds = [forcing[pl.ds(at, 1), :] for at in ats]
            for n in range(GROUP):
                forcing[pl.ds(ats[n], 1), :] = (
                    olds[n] + adds[pl.ds((start + n) * NDEV + s, 1), :]
                )

    own_f[...] = jnp.zeros(own_f.shape, f32)
    own_a[...] = jnp.zeros(own_a.shape, f32)
    group = iota((8, CW), 1) >> 2

    @pl.loop(0, K, unroll=UNROLL)
    def _(level):
        here = group == level
        turn = 4 * level + 2
        for t in range(TILES):
            at = pl.multiple_of(PAD + level * CL, 8) + 8 * t
            u = vel[pl.ds(pl.multiple_of(at, 8), 8), :]
            v, vn, vs = around(vel, PAD + (K + level) * CL, t, 0.0, 0.0)
            base, um, up, _, _ = parts(u, v)
            vm = -jnp.minimum(vs, 0.0)
            vp = jnp.maximum(vn, 0.0)
            cut = slice(8 * t, 8 * t + 8)
            for f in range(F):
                k = kap[f]
                plane = f * K + level
                a, n, s = around(forcing, PAD + 2 * ROWS + plane * CL, t, 0.0, 0.0)
                own_f[f, cut, :] = jnp.where(here, pltpu.roll(a, turn, axis=1), own_f[f, cut, :])
                to = pl.ds(pl.multiple_of(PAD + ROWS + plane * CL + 8 * t, 8), 8)
                more = forcing[to, :]
                own_a[f, cut, :] = jnp.where(here, pltpu.roll(more, turn, axis=1), own_a[f, cut, :])
                b = (
                    (base - 4.0 * k) * a
                    + jnp.where(first, 0.0, west((k + um) * a))
                    + jnp.where(last, 0.0, east((k + up) * a))
                    + (k + vm) * s
                    + (k + vp) * n
                    + more
                )
                forcing[to, :] = b

    for n, at, inner in ((NORTH, CL, CL - 1), (SOUTH, EXT - 1, 0)):
        hu, hv = halo[n, span(F), :], halo[n, span(F + 1), :]
        base, um, up, vm, vp = parts(hu, hv)
        nearest = line(vel, inner, 1)
        push = jnp.maximum(nearest, 0.0) if n == SOUTH else -jnp.minimum(nearest, 0.0)
        on = vp if n == SOUTH else vm
        for f in range(F):
            k = kap[f]
            b = (k + push) * line(forcing, inner, f, 2 * ROWS)
            if n == SOUTH:
                b = jnp.where(bottom, 0.0, b)
            edge[n // 2, span(f), :] = b
            near = (
                (base - 4.0 * k) * b
                + jnp.where(first_k, 0.0, west((k + um) * b))
                + jnp.where(last_k, 0.0, east((k + up) * b))
                + (k + push) * line(forcing, inner, f, ROWS)
            )
            for d, rows in ((0, near), (1, (k + on) * b)):
                to = slice(d * PLANES + f * K, d * PLANES + f * K + K)
                mirrored = reverse_lanes(rows)
                mirrored = -mirrored if f in FLIPPED else mirrored
                if n == NORTH:
                    pay1[to, :] = rows
                    pay2[to, :] = jnp.where(top, mirrored, rows)
                else:
                    pay1[to, :] = jnp.where(odd, rows, pay1[to, :])
                    pay2[to, :] = jnp.where(odd, pay2[to, :], rows)

    base, um, up, vm, vp = parts(side[F], side[F + 1])
    obase, oum, oup, ovm, ovp = parts(mine_all[F], mine_all[F + 1])
    gone = bottom & (iota((EXT, CW), 0) >= CL + 2)
    ends = []
    for f in range(F):
        k = kap[f]
        a = own_f[f]
        oa, ob = (k + oum) * a, (k + oup) * a
        b = jnp.where(slot == 1, east(ob), jnp.where(slot == 2, west(oa), 0.0))
        a = (
            (obase - 4.0 * k) * a
            + jnp.where(slot == 1, west(oa), east(ob))
            + south((k + ovm) * a)
            + north((k + ovp) * a)
        )
        a = jnp.where(gone, 0.0, a) + own_a[f]
        pa = (k + um) * b
        pb = (k + up) * b
        beside1[f] = swapped(jnp.where(slot == 1, pa, pb), slot)
        inner = (
            (base - 4.0 * k) * b
            + south((k + vm) * b)
            + north((k + vp) * b)
            + jnp.where(slot == 1, east((k + oup) * a), west((k + oum) * a))
        )
        outer = jnp.where(slot == 0, east(pb), west(pa))
        beyond = jnp.where((slot == 1) | (slot == 2), inner, outer)
        spill[f] = beyond[:CL]
        ends.append(beyond[CL:])
    post_corners(
        replies,
        [
            corner_rows(ends, 0, 2),
            corner_rows(ends, 0, 1),
            corner_rows(ends, 7, 2),
            corner_rows(ends, 7, 1),
        ],
        bottom,
    )

    def step(level):
        turn = 126 - 4 * level
        for t in range(TILES):
            at = pl.multiple_of(PAD + level * CL, 8) + 8 * t
            u = vel[pl.ds(pl.multiple_of(at, 8), 8), :]
            v, vn, vs = around(
                vel,
                PAD + (K + level) * CL,
                t,
                halo[NORTH, pl.ds((F + 1) * K + level, 1), :],
                halo[SOUTH, pl.ds((F + 1) * K + level, 1), :],
            )
            base, um, up, _, _ = parts(u, v)
            vm = -jnp.minimum(vs, 0.0)
            vp = jnp.maximum(vn, 0.0)
            for f in range(F):
                k = kap[f]
                plane = f * K + level
                start = PAD + ROWS + plane * CL
                a, n, s = around(forcing, start, t, edge_row(0)(plane), edge_row(1)(plane))
                h = pltpu.roll(beside1[f, 8 * t : 8 * t + 8, :], turn, axis=1)
                b = (
                    (base - 4.0 * k) * a
                    + jnp.where(first, h, west((k + um) * a))
                    + jnp.where(last, h, east((k + up) * a))
                    + (k + vm) * s
                    + (k + vp) * n
                    + forcing[pl.ds(pl.multiple_of(PAD + plane * CL + 8 * t, 8), 8), :]
                )
                forcing[pl.ds(pl.multiple_of(PAD + plane * CL + 8 * t, 8), 8), :] = b

    saves = [save]
    for half in range(2):
        pl.loop(half * (K // 2), (half + 1) * (K // 2), unroll=UNROLL)(step)
        for f in range(F):
            at = f * K * CL + half * (K // 2) * CL
            size = K // 2 * CL
            saves.append(
                pltpu.make_async_copy(
                    forcing.at[pl.ds(PAD + at, size)],
                    part.at[pl.ds(at, size)],
                    sems.at[4 + half * F + f],
                )
            )
            saves[-1].start()
    for copy in saves:
        copy.wait()


def finish_kernel(part, from_west, from_east, got1, got2, returned, owner, slots,
                  adjoint, departures, held, sems):
    size = K * CL
    loads, saves = [], []
    for f in range(F):
        cut = pl.ds(f * size, size)
        loads.append(pltpu.make_async_copy(part.at[cut], held.at[cut], sems.at[f]))
        saves.append(pltpu.make_async_copy(held.at[cut], adjoint.at[cut], sems.at[F + f]))
        loads[f].start()

    flat = jnp.transpose(returned[pl.ds(0, NDEV, stride=MESSAGE), :])[:CAP]
    flat = jnp.concatenate(thirds(flat), axis=0)
    dest = iota((NDEV, 128), 0)
    place = iota((CAP, 128), 0).astype(f32)
    for b in range(NBLK):
        hot = (dest == owner[b : b + 1, :]).astype(f32).astype(jnp.bfloat16)
        found = jnp.dot(flat, hot, preferred_element_type=f32)
        found = found[:CAP] + found[CAP : 2 * CAP] + found[2 * CAP :]
        departures[b : b + 1, :] = jnp.sum(
            jnp.where(place == slots[b : b + 1, :], found, 0.0), axis=0, keepdims=True
        )

    odd, top, bottom = where_am_i()
    lane = iota((CL, CW), 1)
    slot = lane & 3
    close = (lane < 2) | (lane >= CW - 2)
    for f in range(F):
        merged = jnp.where(slot < 2, from_east[f], from_west[f])
        loads[f].wait()

        @pl.loop(0, K, unroll=K)
        def _(level):
            more = pltpu.roll(merged, 126 - 4 * level, axis=1)
            at = pl.multiple_of((f * K + level) * CL, CL)
            held[pl.ds(at, CL), :] = held[pl.ds(at, CL), :] + jnp.where(close, more, 0.0)

        north_line = corner_line(returned, f, NE, NW)
        north_line = jnp.where(top, -north_line, north_line) if f in FLIPPED else north_line
        south_line = jnp.where(bottom, 0.0, corner_line(returned, f, SE, SW))
        for d in range(2):
            cut = slice(d * PLANES + f * K, d * PLANES + f * K + K)
            more_up = jnp.where(odd, got2[cut, :], got1[cut, :])
            more_down = jnp.where(odd, got1[cut, :], got2[cut, :])
            if d == 0:
                more_up = more_up + jnp.where(close, spread(north_line), 0.0)
                more_down = more_down + jnp.where(close, spread(south_line), 0.0)
            up = pl.ds(f * size + CL - 1 - d, K, stride=CL)
            held[up, :] = held[up, :] + more_up
            down = pl.ds(f * size + d, K, stride=CL)
            held[down, :] = held[down, :] + more_down
        saves[f].start()
    for copy in saves:
        copy.wait()


def all_to_all(x):
    shape = x.shape
    x = x.reshape(NDEV, 1, MESSAGE * CW)
    x = lax.all_to_all(x, ("lon", "lat"), split_axis=0, concat_axis=0, tiled=True)
    return x.reshape(shape)


def shards(
    background, velocity, diffusivity, obs_value, obs_weight, obs_owner, obs_counts, obs_cell
):
    nlon = lax.axis_size("lon")
    nlat = lax.axis_size("lat")
    both = ("lon", "lat")

    def number(i, j):
        return i * nlat + j

    pairs1 = [(number(i, j), number(i, j ^ 1)) for i in range(nlon) for j in range(nlat)]
    pairs2 = []
    for i in range(nlon):
        for j in range(1, nlat - 1):
            pairs2.append((number(i, j), number(i, j + 1 if j & 1 else j - 1)))
        pairs2.append((number(i, nlat - 1), number(nlon - 1 - i, nlat - 1)))
    eastward = [(i, (i + 1) % nlon) for i in range(nlon)]
    westward = [((i + 1) % nlon, i) for i in range(nlon)]

    def around(x):
        return lax.ppermute(x, "lon", eastward), lax.ppermute(x, "lon", westward)

    x = background.reshape(ROWS, CW)
    vel = velocity.reshape(2 * K * CL, CW)
    own, pay1, pay2 = call(
        edges_kernel,
        [((F + 2, CL, CW), f32)] + [((ALL + PLANES, CW), f32)] * 2,
        [(H, x), (H, vel)],
        "edges",
        scratch=[V((ALL * CL, CW), f32), pltpu.SemaphoreType.DMA((F + 2,))],
    )
    got2 = lax.ppermute(pay2, both, pairs2)
    from_west, from_east = around(own)

    owner = obs_owner.reshape(NBLK, 128)
    packed, slots = call(
        pack_kernel,
        [((MESSAGE * NDEV, CW), f32), ((NBLK, 128), f32)],
        [
            (S, obs_counts),
            (V, obs_value.reshape(NBLK, 128)),
            (V, obs_weight.reshape(NBLK, 128)),
            (V, owner),
            (V, obs_cell.reshape(NBLK, 128)),
            (V, own),
        ],
        "pack",
    )
    pay1, packed = lax.optimization_barrier((pay1, packed))
    got1 = lax.ppermute(pay1, both, pairs1)
    arrived = all_to_all(packed)
    padded = 3 * ROWS + 2 * PAD
    replies, forecast, part, pay1, pay2, spill = call(
        core_kernel,
        [
            ((MESSAGE * NDEV, CW), f32),
            ((ROWS, CW), f32, H),
            ((ROWS, CW), f32, H),
            ((2 * PLANES, CW), f32),
            ((2 * PLANES, CW), f32),
            ((F, CL, CW), f32),
        ],
        [
            (S, diffusivity),
            (V, arrived),
            (H, x),
            (H, vel),
            (V, got1),
            (V, got2),
            (V, own),
            (V, from_west),
            (V, from_east),
        ],
        "core",
        vmem=52,
        scratch=[
            V((padded, CW), f32),
            V((padded, CW), f32),
            V((2 * K * CL + 2 * PAD, CW), f32),
            V((CAP * NDEV, CW), f32),
            V((CAP * NDEV, CW), f32),
            V((CAP * NDEV, CW), i32),
            V((CAP, 128), i32),
            S((CAP, 128), i32),
            V((4, ALL, CW), f32),
            V((2, PLANES, CW), f32),
            V((F + 2, EXT, CW), f32),
            V((F + 2, EXT, CW), f32),
            V((F, EXT, CW), f32),
            V((F, EXT, CW), f32),
            V((F, EXT, CW), f32),
            V((F, EXT, CW), f32),
            pltpu.SemaphoreType.DMA((4 + 2 * F,)),
        ],
    )
    back2 = lax.ppermute(pay2, both, pairs2)
    back1 = lax.ppermute(pay1, both, pairs1)
    spill_west, spill_east = around(spill)
    returned = all_to_all(replies)
    adjoint, found = call(
        finish_kernel,
        [((ROWS, CW), f32, H), ((NBLK, 128), f32)],
        [
            (H, part),
            (V, spill_west),
            (V, spill_east),
            (V, back1),
            (V, back2),
            (V, returned),
            (V, owner),
            (V, slots),
        ],
        "finish",
        scratch=[V((ROWS, CW), f32), pltpu.SemaphoreType.DMA((2 * F,))],
    )
    shape = (F, K, CL, CW)
    return forecast.reshape(shape), adjoint.reshape(shape), found.reshape(-1)


def solution(mesh):
    in_specs = (
        P(None, None, "lat", "lon"),
        P(None, None, "lat", "lon"),
        P(),
        P(("lon", "lat")),
        P(("lon", "lat")),
        P(("lon", "lat"), None),
        P(("lon", "lat"), None),
        P(("lon", "lat")),
    )
    out_specs = (P(None, None, "lat", "lon"), P(None, None, "lat", "lon"), P(("lon", "lat")))
    return jax.shard_map(shards, mesh=mesh, in_specs=in_specs, out_specs=out_specs, check_vma=False)
```
